32 devices in a mesh: hx: 4 (over z), hy: 4 (over x, core), ga: 2 (over y).
Axes of the slice: x: 2, y: 2, z: 4, core: 2. Of those that a mesh axis runs over, the one named last changes fastest.
Arguments:
- density: float32 [32, 128, 256], P('hx', 'hy', 'ga'), may hold values from 0.5 to 2
- velocity: float32 [3, 32, 128, 256], P(None, 'hx', 'hy', 'ga'), may hold values from -3 to 3
- pressure: float32 [32, 128, 256], P('hx', 'hy', 'ga'), may hold values from 0.3 to 3
- species: float32 [9, 32, 128, 256], P(None, 'hx', 'hy', 'ga'), may hold values from 0.05 to 1
- newton_count: int32 [32, 128, 256], P('hx', 'hy', 'ga'), may hold values from 1 to 4
Outputs:
- new_density: float32 [32, 128, 256], P('hx', 'hy', 'ga')
- momentum: float32 [3, 32, 128, 256], P(None, 'hx', 'hy', 'ga')
- total_energy: float32 [32, 128, 256], P('hx', 'hy', 'ga')
- species_mass: float32 [9, 32, 128, 256], P(None, 'hx', 'hy', 'ga')
- potential: float32 [32, 128, 256], P('hx', 'hy', 'ga')
The draws below stay inside these ranges and needn't reach their ends.
Inputs may be any that keep to these rules, and one draw needn't show every extreme that they name: `newton_count`: how many Newton iterations each cell takes.
All inputs are finite; a program needn't handle non-finite values.
Results may differ from the reference program's by a relative error of at most 0.0003.
Values sent between devices are 32-bit elements; how exact they have to be, the bound alone decides.
No kernel may reach another device: no remote copies, remote signals or barrier semaphores. Data moves between devices by JAX's collectives and lax.ppermute only.
A program may use at most 128 MiB of HBM per device.

```python
import math
import jax
import jax.numpy as jnp
from jax import lax

BX = 8
NEWTON = 4
NX = 32
NY = 128
NZ = 256
N_HX = 4


def place_ends(entries, rng, smallest, largest):
    shape = entries.shape
    spot = [jax.random.randint(jax.random.fold_in(rng, axis), (), 0, shape[axis]) for axis in range(len(shape))]
    entries = entries.at[tuple(spot)].set(smallest)
    longest = shape.index(max(shape))
    spot[longest] = (spot[longest] + 1) % shape[longest]
    return entries.at[tuple(spot)].set(largest)


def steps_of(rng, shape, pieces, least, largest):
    loudness, own = 1.0, jax.random.fold_in(rng, 6)
    for position, blocks in pieces:
        steps = jnp.exp(jax.random.uniform(jax.random.fold_in(own, position), (blocks,), jnp.float32, least / len(pieces), largest / len(pieces)))
        loudness = loudness * jnp.repeat(steps, shape[position] // blocks).reshape([-1 if axis == position else 1 for axis in range(len(shape))])
    return loudness


def gaussian(key, shape, scale, reach, shards=(), kind=jnp.bfloat16):
    gain = steps_of(key, shape, shards, -0.22, 0.18) if shards else 1.0
    entries = jax.random.normal(key, shape, jnp.float32) * scale * gain
    return jnp.minimum(jnp.maximum(entries, -reach), reach).astype(kind)


def setup_inputs(seed: int = 0) -> dict:
    seeds = jax.random.split(jax.random.key(seed), 6)
    density = jnp.clip(jnp.exp(math.log(2.0) - 1.3862944 * jax.random.uniform(seeds[0], (NX, NY, NZ), jnp.float32) ** steps_of(seeds[0], (NX, NY, NZ), ((0, 4), (1, 4), (2, 2)), -0.2, 0.2)), 0.5, 2.0)
    velocity = gaussian(seeds[1], (3, NX, NY, NZ), 0.5, 3.0, ((1, 4), (2, 4), (3, 2)), jnp.float32)
    pressure = jnp.clip(jnp.exp(math.log(3.0) - 2.3025851 * jax.random.uniform(seeds[2], (NX, NY, NZ), jnp.float32) ** steps_of(seeds[2], (NX, NY, NZ), ((0, 4), (1, 4), (2, 2)), -0.2, 0.2)), 0.3, 3.0)
    species = jnp.clip(0.05 + 0.95 * jax.random.uniform(seeds[3], (9, NX, NY, NZ), jnp.float32) ** steps_of(seeds[3], (9, NX, NY, NZ), ((1, 4), (2, 4), (3, 2)), -0.2, 0.2), 0.05, 1.0)
    newton_count = place_ends(jax.random.randint(seeds[4], (NX, NY, NZ), 1, 5), jax.random.fold_in(seeds[4], 1), 1, 4).astype(jnp.int32)
    return {"density": density, "velocity": velocity, "pressure": pressure, "species": species, "newton_count": newton_count}


gamma_gas = 5.0 / 3.0
time_step = 0.1
cool_rates = (2.0, 5.0, 9.0, 14.0, 20.0, 3.0, 7.0, 11.0, 29.0)

def cooled_pressure(density, pressure, species, newton_count):
    cooling = cool_rates[0] * species[0]
    for species_index in range(1, 9):
        cooling = cooling + cool_rates[species_index] * species[species_index]
    stiffness = time_step * density * cooling
    initial = pressure / ((gamma_gas - 1.0) * density)
    energy = initial
    for newton_step in range(NEWTON):
        residual_value = energy - initial + stiffness * energy * energy / (1.0 + energy)
        derivative = 1.0 + stiffness * energy * (energy + 2.0) / ((1.0 + energy) * (1.0 + energy))
        energy = jnp.where(newton_count > newton_step, energy - residual_value / derivative, energy)
    return (gamma_gas - 1.0) * density * energy

def conserved(primitive):
    density = primitive[0]
    velocity = primitive[1:4]
    kinetic = 0.5 * density * (velocity[0] * velocity[0] + velocity[1] * velocity[1] + velocity[2] * velocity[2])
    energy = primitive[4] / (gamma_gas - 1.0) + kinetic
    return jnp.concatenate([density[None], density[None] * velocity, energy[None], density[None] * primitive[5:14]], axis=0)

def face_flux(lower_cells, upper_cells, direction):
    sides_data = []
    for side_cells in (lower_cells, upper_cells):
        amounts = conserved(side_cells)
        normal = side_cells[1 + direction]
        carried = amounts * normal[None]
        carried = carried.at[1 + direction].add(side_cells[4])
        carried = carried.at[4].add(side_cells[4] * normal)
        signal = jnp.abs(normal) + jnp.sqrt(gamma_gas * side_cells[4] / side_cells[0])
        sides_data.append((amounts, carried, signal))
    wave_speed = jnp.maximum(sides_data[0][2], sides_data[1][2])
    return 0.5 * (sides_data[0][1] + sides_data[1][1]) - 0.5 * wave_speed[None] * (sides_data[1][0] - sides_data[0][0])

def window(padded, array_axis, offset, extent):
    selection = [slice(None), slice(1, -1), slice(1, -1), slice(1, -1)]
    selection[array_axis] = slice(offset, offset + extent)
    return padded[tuple(selection)]

def advance(padded):
    primitive = padded[0:14]
    current = conserved(primitive[:, 1:-1, 1:-1, 1:-1])
    change = jnp.zeros_like(current)
    accelerations = []
    for direction in range(3):
        array_axis = 1 + direction
        extent = current.shape[array_axis]
        across = face_flux(window(primitive, array_axis, 0, extent + 1), window(primitive, array_axis, 1, extent + 1), direction)
        change = change + (lax.slice_in_dim(across, 1, extent + 1, axis=array_axis) - lax.slice_in_dim(across, 0, extent, axis=array_axis))
        accelerations.append(-0.5 * (window(padded[14:15], array_axis, 2, extent) - window(padded[14:15], array_axis, 0, extent))[0])
    updated = current - time_step * change
    density = current[0]
    momentum = jnp.concatenate([(updated[1 + direction] + time_step * density * accelerations[direction])[None] for direction in range(3)], axis=0)
    energy = updated[4] + time_step * (current[1] * accelerations[0] + current[2] * accelerations[1] + current[3] * accelerations[2])
    return (updated[0], momentum, energy, updated[5:14])

def eigenvalues(extent):
    waves = jnp.arange(extent).astype(jnp.float32)
    return 2.0 * jnp.cos(2.0 * jnp.pi / extent * waves) - 2.0

def solve_potential(density):
    total = eigenvalues(NX)[:, None, None] + eigenvalues(NY)[None, :, None] + eigenvalues(NZ)[None, None, :]
    green = jnp.where(total < 0.0, 1.0 / jnp.where(total < 0.0, total, -1.0), 0.0)
    return jnp.fft.ifftn(jnp.fft.fftn(density) * green).real

def reference(density, velocity, pressure, species, newton_count):
    potential = solve_potential(density)

    def one_block(block_number):
        rows_taken = (block_number * BX - 1 + jnp.arange(BX + 2, dtype=jnp.int32)) % NX

        def take_rows(field):
            return jnp.take(field, rows_taken, axis=field.ndim - 3)
        density_rows = take_rows(density)
        species_rows = take_rows(species)
        cooled = cooled_pressure(density_rows, take_rows(pressure), species_rows, take_rows(newton_count))
        gas_stack = jnp.concatenate([density_rows[None], take_rows(velocity), cooled[None], species_rows, take_rows(potential)[None]], axis=0)
        padded = jnp.pad(gas_stack, ((0, 0), (0, 0), (1, 1), (1, 1)), mode='wrap')
        return advance(padded)
    results = lax.map(one_block, jnp.arange(N_HX, dtype=jnp.int32))
    new_density = results[0].reshape(NX, NY, NZ)
    momentum = jnp.moveaxis(results[1], 1, 0).reshape(3, NX, NY, NZ)
    total_energy = results[2].reshape(NX, NY, NZ)
    species_mass = jnp.moveaxis(results[3], 1, 0).reshape(9, NX, NY, NZ)
    return (new_density, momentum, total_energy, species_mass, potential)
```

```python
import functools
import math

import jax
import jax.numpy as jnp
import numpy as np
from jax import lax
from jax.experimental import pallas as pl
from jax.experimental.pallas import tpu as pltpu
from jax.sharding import PartitionSpec as P

NEWTON = 4
gamma_gas = 5.0 / 3.0
time_step = 0.1
cool_rates = (2.0, 5.0, 9.0, 14.0, 20.0, 3.0, 7.0, 11.0, 29.0)
species_n = len(cool_rates)
prim_n = 5 + species_n
half_step = 0.5 * time_step
highest = lax.Precision.HIGHEST
LANES = 128
P_AT = prim_n
C_AT = prim_n + 1
V_AT = prim_n + 2
field_n = prim_n + 5
face_n = prim_n + 3
HIGH_FACE = 64


def fields_of(primitive):
    density, v0, v1, v2, pressure = primitive[:5]
    energy = pressure * (1.0 / (gamma_gas - 1.0)) + 0.5 * density * (v0 * v0 + v1 * v1 + v2 * v2)
    sound = jnp.sqrt(gamma_gas * pressure / density)
    return (
        [density, density * v0, density * v1, density * v2, energy]
        + list(primitive[5:])
        + [pressure, sound, v0, v1, v2]
    )


def cooled_plane(density, pressure, species, count):
    cooling = cool_rates[0] * species[0]
    for s in range(1, species_n):
        cooling = cooling + cool_rates[s] * species[s]
    stiffness = time_step * density * cooling
    initial = pressure / ((gamma_gas - 1.0) * density)
    energy = initial
    for step in range(NEWTON):
        above = 1.0 + energy
        residual = ((energy - initial) * above + stiffness * energy * energy) * above
        derivative = above * above + stiffness * energy * (energy + 2.0)
        energy = jnp.where(count > step, energy - residual / derivative, energy)
    return (gamma_gas - 1.0) * density * energy


def pack_kernel(den, vel, pre, spe, cnt, cooled, xlo, xhi, ylo, yhi, zface):
    nx, ny, nz = den.shape
    lane = lax.broadcasted_iota(jnp.int32, (ny, LANES), 1)

    def plane(x, _):
        density = den[x]
        species = [spe[s, x] for s in range(species_n)]
        pressure = cooled_plane(density, pre[x], species, cnt[x])
        cooled[x] = pressure
        primitive = [density, vel[0, x], vel[1, x], vel[2, x], pressure] + [density * s for s in species]
        for c in range(prim_n):
            ylo[c, pl.ds(x, 1), :] = primitive[c][0:1, :]
            yhi[c, pl.ds(x, 1), :] = primitive[c][ny - 1 : ny, :]

        @pl.when(x == 0)
        def _():
            for c in range(prim_n):
                xlo[c] = primitive[c]

        @pl.when(x == nx - 1)
        def _():
            for c in range(prim_n):
                xhi[c] = primitive[c]

        fields = fields_of(primitive)
        carried = fields[: C_AT + 1] + [fields[V_AT + 2]]
        packed = jnp.zeros((ny, LANES), jnp.float32)
        for c in range(face_n):
            first, last = carried[c][:, :LANES], carried[c][:, nz - LANES :]
            packed = jnp.where(lane == c, pltpu.roll(first, c, 1) if c else first, packed)
            packed = jnp.where(lane == HIGH_FACE + c, pltpu.roll(last, HIGH_FACE + c + 1, 1), packed)
        zface[x] = packed
        return 0

    lax.fori_loop(0, nx, plane, 0)


def flux_kernel(den, vel, cooled, spe, xbelow, xabove, ybelow, yabove, zbelow, zabove,
                new_density, momentum, energy, mass, ext, yedge):
    nx, ny, nz = den.shape
    row = lax.broadcasted_iota(jnp.int32, (ny, nz), 0)
    lane = lax.broadcasted_iota(jnp.int32, (ny, nz), 1)

    for side, (at, face) in enumerate(((0, xbelow), (nx + 1, xabove))):
        for f, value in enumerate(fields_of([face[c] for c in range(prim_n)])):
            ext[f, at] = value
    for side, face in enumerate((ybelow, yabove)):
        for f, value in enumerate(fields_of([face[c] for c in range(prim_n)])):
            yedge[side, f] = value

    def derive(x, _):
        density = den[x]
        primitive = [density, vel[0, x], vel[1, x], vel[2, x], cooled[x]]
        primitive += [density * spe[s, x] for s in range(species_n)]
        for f, value in enumerate(fields_of(primitive)):
            ext[f, x + 1] = value
        return 0

    lax.fori_loop(0, nx, derive, 0)

    def plane(x, _):
        from_below = zbelow[x]
        from_above = zabove[x]

        def beside(f, direction, up):
            if direction == 0:
                return ext[f, x + 2] if up else ext[f, x]
            here = ext[f, x + 1]
            if direction == 1:
                edge = yedge[1 if up else 0, f, pl.ds(x, 1), :]
                if up:
                    return jnp.where(row == ny - 1, edge, pltpu.roll(here, ny - 1, 0))
                return jnp.where(row == 0, edge, pltpu.roll(here, 1, 0))
            slot = f if f < V_AT else prim_n + 2
            if up:
                edge = pltpu.roll(from_above, LANES - 1 - slot, 1)
                return jnp.where(lane == nz - 1, edge, pltpu.roll(here, nz - 1, 1))
            edge = pltpu.roll(from_below, LANES - HIGH_FACE - slot, 1)
            return jnp.where(lane == 0, edge, pltpu.roll(here, 1, 1))

        sound = ext[C_AT, x + 1]
        centre = 1.0
        above, below, push, work = [], [], [], 0.0
        for d in range(3):
            speed = jnp.abs(ext[V_AT + d, x + 1]) + sound
            v_up, v_lo = beside(V_AT + d, d, True), beside(V_AT + d, d, False)
            p_up, p_lo = beside(P_AT, d, True), beside(P_AT, d, False)
            s_up = jnp.maximum(speed, jnp.abs(v_up) + beside(C_AT, d, True))
            s_lo = jnp.maximum(speed, jnp.abs(v_lo) + beside(C_AT, d, False))
            centre = centre - half_step * (s_up + s_lo)
            above.append(half_step * (s_up - v_up))
            below.append(half_step * (s_lo + v_lo))
            push.append(half_step * (p_lo - p_up))
            work = work + half_step * (p_lo * v_lo - p_up * v_up)

        def updated(f):
            total = centre * ext[f, x + 1]
            for d in range(3):
                total = total + above[d] * beside(f, d, True)
                total = total + below[d] * beside(f, d, False)
            return total

        new_density[x] = updated(0)
        for d in range(3):
            momentum[d, x] = updated(1 + d) + push[d]
        energy[x] = updated(4) + work
        for s in range(species_n):
            mass[s, x] = updated(5 + s)
        return 0

    lax.fori_loop(0, nx, plane, 0)


def vmem_call(kernel, out_shape, **more):
    return pl.pallas_call(
        kernel,
        out_shape=[jax.ShapeDtypeStruct(s, jnp.float32) for s in out_shape],
        **more,
    )


def shifted(value, axis, step):
    count = lax.axis_size(axis)
    return lax.ppermute(value, axis, [(i, (i + step) % count) for i in range(count)])


def hartley(row_keys, col_keys, length):
    phase = row_keys[:, None] * col_keys[None, :] % length
    angle = 2.0 * jnp.pi / length * phase.astype(jnp.float32)
    return jnp.cos(angle) + jnp.sin(angle)


def eigen_keys(keys, extent):
    return 2.0 * jnp.cos(2.0 * jnp.pi / extent * keys.astype(jnp.float32)) - 2.0


def spectral_solve(planes_data, wave_y, total_y):
    total_x = planes_data.shape[0]
    total_z = planes_data.shape[2]
    keys_x = jnp.arange(total_x, dtype=jnp.int32)
    keys_z = jnp.arange(total_z, dtype=jnp.int32)
    table_x = hartley(keys_x, keys_x, total_x)
    table_z = hartley(keys_z, keys_z, total_z)
    turned = jnp.einsum("ab,byz->ayz", table_x, planes_data, precision=highest)
    turned = jnp.einsum("ayz,zc->ayc", turned, table_z, precision=highest)
    total = (
        eigen_keys(keys_x, total_x)[:, None, None]
        + eigen_keys(wave_y, total_y)[None, :, None]
        + eigen_keys(keys_z, total_z)[None, None, :]
    )
    green = jnp.where(total < 0.0, 1.0 / jnp.where(total < 0.0, total, -1.0), 0.0) / (
        total_x * total_y * total_z
    )
    turned = turned * green
    turned = jnp.einsum("ab,byz->ayz", table_x, turned, precision=highest)
    return jnp.einsum("ayz,zc->ayc", turned, table_z, precision=highest)


def local(density, velocity, pressure, species, newton_count):
    size_x = lax.axis_size("hx")
    size_y = lax.axis_size("hy")
    size_g = lax.axis_size("ga")
    rank_x = lax.axis_index("hx")
    rank_y = lax.axis_index("hy")
    rank_g = lax.axis_index("ga")
    rows_y = density.shape[1]
    total_y = rows_y * size_y
    slab_share = rows_y // size_x
    thin_rows = slab_share // size_g
    keys_y = jnp.arange(total_y, dtype=jnp.int32)
    local_keys = jnp.arange(thin_rows, dtype=jnp.int32)
    table_y = hartley(keys_y, keys_y, total_y)
    gathered = lax.all_to_all(density, "hy", split_axis=0, concat_axis=1, tiled=True)
    turned = jnp.einsum("ab,xbz->xaz", table_y, gathered, precision=highest)
    planes_data = lax.all_to_all(
        lax.all_to_all(turned, ("hx", "hy"), split_axis=1, concat_axis=0, tiled=True),
        "ga",
        split_axis=1,
        concat_axis=2,
        tiled=True,
    )
    wave_y = (rank_x * size_y + rank_y) * slab_share + rank_g * thin_rows + local_keys
    solved = spectral_solve(planes_data, wave_y, total_y)
    returned = lax.all_to_all(
        lax.all_to_all(solved, ("hx", "hy"), split_axis=0, concat_axis=1, tiled=True),
        "ga",
        split_axis=2,
        concat_axis=1,
        tiled=True,
    )
    from_group = keys_y // (thin_rows * size_x * size_y)
    remainder = keys_y % (thin_rows * size_x * size_y)
    column_keys = (
        remainder // thin_rows * slab_share + from_group * thin_rows + remainder % thin_rows
    )
    inverted = jnp.einsum(
        "ab,xbz->xaz", hartley(keys_y, column_keys, total_y), returned, precision=highest
    )
    potential = lax.all_to_all(inverted, "hy", split_axis=1, concat_axis=0, tiled=True)
    nx, ny, nz = density.shape
    cooled, xlo, xhi, ylo, yhi, zface = vmem_call(
        pack_kernel,
        [(nx, ny, nz)] + [(prim_n, ny, nz)] * 2 + [(prim_n, nx, nz)] * 2 + [(nx, ny, LANES)],
    )(density, velocity, pressure, species, newton_count)
    xbelow, xabove = shifted(xhi, "hx", 1), shifted(xlo, "hx", -1)
    ybelow, yabove = shifted(yhi, "hy", 1), shifted(ylo, "hy", -1)
    zbelow = shifted(zface, "ga", 1)
    zabove = zbelow if size_g == 2 else shifted(zface, "ga", -1)
    new_density, momentum, total_energy, species_mass = vmem_call(
        flux_kernel,
        [(nx, ny, nz), (3, nx, ny, nz), (nx, ny, nz), (species_n, nx, ny, nz)],
        scratch_shapes=[
            pltpu.VMEM((field_n, nx + 2, ny, nz), jnp.float32),
            pltpu.VMEM((2, field_n, nx, nz), jnp.float32),
        ],
    )(density, velocity, cooled, species, xbelow, xabove, ybelow, yabove, zbelow, zabove)
    gravity = []
    for d, axis in enumerate(("hx", "hy", "ga")):
        n = potential.shape[d]
        first = lax.slice_in_dim(potential, 0, 1, axis=d)
        last = lax.slice_in_dim(potential, n - 1, n, axis=d)
        wide = jnp.concatenate([shifted(last, axis, 1), potential, shifted(first, axis, -1)], axis=d)
        gravity.append(
            -0.5 * (lax.slice_in_dim(wide, 2, n + 2, axis=d) - lax.slice_in_dim(wide, 0, n, axis=d))
        )
    kick = time_step * density * jnp.stack(gravity)
    return (
        new_density,
        momentum + kick,
        total_energy + jnp.sum(kick * velocity, axis=0),
        species_mass,
        potential,
    )


def solution(mesh):
    in_specs = (
        P("hx", "hy", "ga"),
        P(None, "hx", "hy", "ga"),
        P("hx", "hy", "ga"),
        P(None, "hx", "hy", "ga"),
        P("hx", "hy", "ga"),
    )
    out_specs = (
        P("hx", "hy", "ga"),
        P(None, "hx", "hy", "ga"),
        P("hx", "hy", "ga"),
        P(None, "hx", "hy", "ga"),
        P("hx", "hy", "ga"),
    )
    return jax.shard_map(local, mesh=mesh, in_specs=in_specs, out_specs=out_specs, check_vma=False)
```

```python
import functools
import math

import jax
import jax.numpy as jnp
import numpy as np
from jax import lax
from jax.experimental import pallas as pl
from jax.experimental.pallas import tpu as pltpu
from jax.sharding import PartitionSpec as P

NEWTON = 4
gamma_gas = 5.0 / 3.0
time_step = 0.1
cool_rates = (2.0, 5.0, 9.0, 14.0, 20.0, 3.0, 7.0, 11.0, 29.0)
species_n = len(cool_rates)
prim_n = 5 + species_n
half_step = 0.5 * time_step
highest = lax.Precision.HIGHEST
LANES = 128
P_AT = prim_n
C_AT = prim_n + 1
V_AT = prim_n + 2
field_n = prim_n + 5
face_n = prim_n + 3
HIGH_FACE = 64


def fields_of(primitive):
    density, v0, v1, v2, pressure = primitive[:5]
    energy = pressure * (1.0 / (gamma_gas - 1.0)) + 0.5 * density * (v0 * v0 + v1 * v1 + v2 * v2)
    sound = jnp.sqrt(gamma_gas * pressure / density)
    return (
        [density, density * v0, density * v1, density * v2, energy]
        + list(primitive[5:])
        + [pressure, sound, v0, v1, v2]
    )


def cooled_plane(density, pressure, species, count):
    cooling = cool_rates[0] * species[0]
    for s in range(1, species_n):
        cooling = cooling + cool_rates[s] * species[s]
    stiffness = time_step * density * cooling
    initial = pressure / ((gamma_gas - 1.0) * density)
    energy = initial
    for step in range(NEWTON):
        above = 1.0 + energy
        residual = ((energy - initial) * above + stiffness * energy * energy) * above
        derivative = above * above + stiffness * energy * (energy + 2.0)
        energy = jnp.where(count > step, energy - residual / derivative, energy)
    return (gamma_gas - 1.0) * density * energy


def pack_kernel(den, vel, pre, spe, cnt, cooled, xlo, xhi, ylo, yhi, zface):
    nx, ny, nz = den.shape
    lane = lax.broadcasted_iota(jnp.int32, (ny, LANES), 1)

    def plane(x, _):
        density = den[x]
        species = [spe[s, x] for s in range(species_n)]
        pressure = cooled_plane(density, pre[x], species, cnt[x])
        cooled[x] = pressure
        primitive = [density, vel[0, x], vel[1, x], vel[2, x], pressure] + [density * s for s in species]
        for c in range(prim_n):
            ylo[c, pl.ds(x, 1), :] = primitive[c][0:1, :]
            yhi[c, pl.ds(x, 1), :] = primitive[c][ny - 1 : ny, :]

        @pl.when(x == 0)
        def _():
            for c in range(prim_n):
                xlo[c] = primitive[c]

        @pl.when(x == nx - 1)
        def _():
            for c in range(prim_n):
                xhi[c] = primitive[c]

        fields = fields_of(primitive)
        carried = fields[: C_AT + 1] + [fields[V_AT + 2]]
        packed = jnp.zeros((ny, LANES), jnp.float32)
        for c in range(face_n):
            first, last = carried[c][:, :LANES], carried[c][:, nz - LANES :]
            packed = jnp.where(lane == c, pltpu.roll(first, c, 1) if c else first, packed)
            packed = jnp.where(lane == HIGH_FACE + c, pltpu.roll(last, HIGH_FACE + c + 1, 1), packed)
        zface[x] = packed
        return 0

    lax.fori_loop(0, nx, plane, 0)


def flux_kernel(den, vel, cooled, spe, xbelow, xabove, ybelow, yabove, zbelow, zabove,
                new_density, momentum, energy, mass, ext, yedge):
    nx, ny, nz = den.shape
    row = lax.broadcasted_iota(jnp.int32, (ny, nz), 0)
    lane = lax.broadcasted_iota(jnp.int32, (ny, nz), 1)

    for side, (at, face) in enumerate(((0, xbelow), (nx + 1, xabove))):
        for f, value in enumerate(fields_of([face[c] for c in range(prim_n)])):
            ext[f, at] = value
    for side, face in enumerate((ybelow, yabove)):
        for f, value in enumerate(fields_of([face[c] for c in range(prim_n)])):
            yedge[side, f] = value

    def derive(x, _):
        density = den[x]
        primitive = [density, vel[0, x], vel[1, x], vel[2, x], cooled[x]]
        primitive += [density * spe[s, x] for s in range(species_n)]
        for f, value in enumerate(fields_of(primitive)):
            ext[f, x + 1] = value
        return 0

    lax.fori_loop(0, nx, derive, 0)

    def plane(x, _):
        from_below = zbelow[x]
        from_above = zabove[x]

        def beside(f, direction, up):
            if direction == 0:
                return ext[f, x + 2] if up else ext[f, x]
            here = ext[f, x + 1]
            if direction == 1:
                edge = yedge[1 if up else 0, f, pl.ds(x, 1), :]
                if up:
                    return jnp.where(row == ny - 1, edge, pltpu.roll(here, ny - 1, 0))
                return jnp.where(row == 0, edge, pltpu.roll(here, 1, 0))
            slot = f if f < V_AT else prim_n + 2
            if up:
                edge = pltpu.roll(from_above, LANES - 1 - slot, 1)
                return jnp.where(lane == nz - 1, edge, pltpu.roll(here, nz - 1, 1))
            edge = pltpu.roll(from_below, LANES - HIGH_FACE - slot, 1)
            return jnp.where(lane == 0, edge, pltpu.roll(here, 1, 1))

        sound = ext[C_AT, x + 1]
        centre = 1.0
        above, below, push, work = [], [], [], 0.0
        for d in range(3):
            speed = jnp.abs(ext[V_AT + d, x + 1]) + sound
            v_up, v_lo = beside(V_AT + d, d, True), beside(V_AT + d, d, False)
            p_up, p_lo = beside(P_AT, d, True), beside(P_AT, d, False)
            s_up = jnp.maximum(speed, jnp.abs(v_up) + beside(C_AT, d, True))
            s_lo = jnp.maximum(speed, jnp.abs(v_lo) + beside(C_AT, d, False))
            centre = centre - half_step * (s_up + s_lo)
            above.append(half_step * (s_up - v_up))
            below.append(half_step * (s_lo + v_lo))
            push.append(half_step * (p_lo - p_up))
            work = work + half_step * (p_lo * v_lo - p_up * v_up)

        def updated(f):
            total = centre * ext[f, x + 1]
            for d in range(3):
                total = total + above[d] * beside(f, d, True)
                total = total + below[d] * beside(f, d, False)
            return total

        new_density[x] = updated(0)
        for d in range(3):
            momentum[d, x] = updated(1 + d) + push[d]
        energy[x] = updated(4) + work
        for s in range(species_n):
            mass[s, x] = updated(5 + s)
        return 0

    lax.fori_loop(0, nx, plane, 0)


def vmem_call(kernel, out_shape, **more):
    return pl.pallas_call(
        kernel,
        out_shape=[jax.ShapeDtypeStruct(s, jnp.float32) for s in out_shape],
        **more,
    )


def shifted(value, axis, step):
    count = lax.axis_size(axis)
    return lax.ppermute(value, axis, [(i, (i + step) % count) for i in range(count)])


def hartley(rows, columns, length):
    angle = 2.0 * np.pi / length * (np.outer(rows, columns) % length)
    return np.cos(angle) + np.sin(angle)


def curvature(length):
    return 4.0 * np.sin(np.pi / length * np.arange(length)) ** 2


def decay_tables(nx, ny, nz):
    mu = curvature(nz)[:, None] + curvature(ny)[None, :]
    mu[0, 0] = 1.0
    root = np.sqrt(mu * (4.0 + mu))
    decay = 2.0 / (2.0 + mu + root)
    return np.stack([decay, 1.0 / (1.0 - decay**nx), -1.0 / (root * ny * nz)]).astype(np.float32)


def flat_mode_table(block, nx, ny, nz):
    rows = -(-(block + 2) // 8) * 8
    cell = np.arange(-1, rows - 1)[:, None]
    segment = np.arange(nx // block)[:, None]
    source = (np.arange(block)[None, :] - block * segment).reshape(1, -1)
    gap = (cell - source) % nx
    table = gap * (nx - gap) / (2.0 * nx) - (nx * nx - 1.0) / (12.0 * nx)
    return (table / (ny * nz)).astype(np.float32)


def along_z_kernel(part, den, table, out):
    nx, ny, nz = den.shape
    out[...] = lax.dot_general(
        table[part[0]], den[...].reshape(nx * ny, nz), (((1,), (1,)), ((), ())),
        precision=highest, preferred_element_type=jnp.float32,
    )


def segments(kz, width):
    return lax.broadcasted_iota(jnp.int32, (kz, LANES), 1) // width


def turned(value, lanes):
    lanes = lanes % LANES
    return pltpu.roll(value, lanes, 1) if lanes else value


def along_y_kernel(size_g, block, parts, lines, table_y, tables, modes, sums, grid_rows):
    groups, kz, _ = lines.shape
    nx, _, ny = modes.shape
    width = block
    per = LANES // width
    place = segments(kz, width)
    for column in range(ny // LANES):
        for high in range(nx // per):
            source = []
            for s in range(per):
                first = (column * per + s) * size_g
                total = lines[first, :, high * LANES : (high + 1) * LANES]
                for g in range(1, size_g):
                    total = total + lines[first + g, :, high * LANES : (high + 1) * LANES]
                source.append(total)
            for low in range(per):
                line = turned(source[0], -low * width)
                for s in range(1, per):
                    line = jnp.where(place == s, turned(source[s], (s - low) * width), line)
                x = high * per + low
                grid_rows[x * kz : (x + 1) * kz, column * LANES : (column + 1) * LANES] = line
    spectrum = jnp.dot(
        grid_rows[...], table_y[...], precision=highest, preferred_element_type=jnp.float32
    )
    modes[...] = spectrum.reshape(nx, kz, ny)
    decay = tables[0, pl.ds(parts[0] * kz, kz), :]
    forward, backward = modes[0], modes[nx - 1]
    for x in range(1, nx):
        forward = forward * decay + modes[x]
        backward = backward * decay + modes[nx - 1 - x]
    sums[0:kz] = forward
    sums[kz : 2 * kz] = backward
    for x in range(nx):
        sums[2 * kz + x : 2 * kz + x + 1] = modes[x, 0:1, :]


def along_x_kernel(count, size_g, block, parts, modes, own, *rest):
    others = rest[: count - 1]
    table_y, tables, flat_table, out, gathered, potential, lines = rest[count - 1 :]
    nx, kz, ny = modes.shape
    width = block
    per = LANES // width
    for s in range(count):
        seen = own if s == 0 else others[s - 1]
        gathered[s * nx : (s + 1) * nx] = seen[2 * kz : 2 * kz + nx]
    flat = jnp.dot(
        flat_table[...], gathered[...], precision=highest, preferred_element_type=jnp.float32
    )
    for tile in range(0, kz, 8):
        rows = slice(tile, tile + 8)
        at = pl.ds(parts[0] * kz + tile, 8)
        decay, closing, scale = tables[0, at, :], tables[1, at, :], tables[2, at, :]
        far = decay
        for _ in range(int(math.log2(nx))):
            far = far * far
        left = own[tile : tile + 8]
        right = own[kz + tile : kz + tile + 8]
        for s in range(count - 1, 0, -1):
            left = left * far + others[s - 1][tile : tile + 8]
            right = right * far + others[count - s - 1][kz + tile : kz + tile + 8]
        left, right = left * closing, right * closing
        from_left = [left]
        for x in range(nx):
            from_left.append(from_left[-1] * decay + modes[x, rows])
        result = [None] * (nx + 2)
        result[nx + 1] = from_left[nx] * decay + right
        behind = right
        for x in range(nx - 1, -1, -1):
            result[x + 1] = behind * decay + from_left[x + 1]
            behind = behind * decay + modes[x, rows]
        result[0] = from_left[0] + behind * decay
        if tile == 0:
            first = lax.broadcasted_iota(jnp.int32, (8, ny), 0) + lax.broadcasted_iota(jnp.int32, (8, ny), 1)
            first = first + parts[0] == 0
        for x in range(nx + 2):
            value = result[x] * scale
            if tile == 0:
                value = jnp.where(first, flat[x : x + 1, :], value)
            potential[x * kz + tile : x * kz + tile + 8] = value
    lines[...] = jnp.dot(
        potential[...], table_y[...], precision=highest, preferred_element_type=jnp.float32
    )
    place = segments(kz, width)
    lane = lax.broadcasted_iota(jnp.int32, (kz, LANES), 1)

    def line(x, column):
        return lines[(x + 1) * kz : (x + 2) * kz, column * LANES : (column + 1) * LANES]

    for target in range(ny // width):
        column, s = target // per, target % per
        pieces = []
        for high in range(nx // per):
            piece = turned(line(high * per, column), -s * width)
            for low in range(1, per):
                piece = jnp.where(place == low, turned(line(high * per + low, column), (low - s) * width), piece)
            pieces.append(piece)
        edge = turned(line(-1, column), -s * width)
        edge = jnp.where(place == 1, turned(line(nx, column), (1 - s) * width), edge)
        for side, y in enumerate((target * width - 1, (target + 1) * width)):
            y = y % ny
            for x in range(nx):
                slot = 2 * width + side * nx + x
                edge = jnp.where(lane == slot, turned(line(x, y // LANES), slot - y % LANES), edge)
        pieces.append(edge)
        for g in range(size_g):
            for p, piece in enumerate(pieces):
                out[target * size_g + g, :, p * LANES : (p + 1) * LANES] = piece


def gravity_kernel(part, planes, table, den, vel, momentum_in, energy_in, potential, momentum, energy, solved, edges):
    nx, ny, nz = den.shape
    groups, kz, width = planes.shape
    main = nx * ny
    flat = planes[...].reshape(groups * kz, width)
    here = table[part[0]]
    contract = (((0,), (0,)), ((), ()))
    solved[...] = lax.dot_general(
        flat[:, :main], here, contract, precision=highest, preferred_element_type=jnp.float32
    )
    edges[...] = lax.dot_general(
        flat[:, main:], here[:, :nz], contract, precision=highest, preferred_element_type=jnp.float32
    )
    row = lax.broadcasted_iota(jnp.int32, (ny, nz), 0)
    for x in range(nx):
        value = solved[x * ny : (x + 1) * ny, :nz]
        potential[x] = value
        above = solved[(x + 1) * ny : (x + 2) * ny, :nz] if x < nx - 1 else edges[ny : 2 * ny]
        below = solved[(x - 1) * ny : x * ny, :nz] if x > 0 else edges[:ny]
        at = 2 * ny + x
        right = jnp.where(row == ny - 1, edges[at + nx : at + nx + 1], pltpu.roll(value, ny - 1, 0))
        left = jnp.where(row == 0, edges[at : at + 1], pltpu.roll(value, 1, 0))
        pull = time_step * den[x]
        kicks = [
            pull * (-0.5 * (above - below)),
            pull * (-0.5 * (right - left)),
            pull * solved[x * ny : (x + 1) * ny, nz:],
        ]
        work = energy_in[x]
        for d in range(3):
            momentum[d, x] = momentum_in[d, x] + kicks[d]
            work = work + kicks[d] * vel[d, x]
        energy[x] = work


def local(density, velocity, pressure, species, newton_count):
    size_x, size_y, size_g = (lax.axis_size(a) for a in ("hx", "hy", "ga"))
    nx, ny, nz = density.shape
    all_x, all_y, all_z = nx * size_x, ny * size_y, nz * size_g
    groups = size_y * size_g
    kz = all_z // groups
    in_g = lax.axis_index("ga").astype(jnp.int32).reshape(1)
    in_plane = (lax.axis_index("hy") * size_g + lax.axis_index("ga")).astype(jnp.int32).reshape(1)
    main = nx * ny
    width = main + LANES

    keys_z = np.arange(all_z)
    table_z = hartley(keys_z, keys_z, all_z)
    ahead = hartley(keys_z, keys_z + 1, all_z)
    behind = hartley(keys_z, keys_z - 1, all_z)
    into_z = jnp.asarray(table_z.reshape(all_z, size_g, nz).transpose(1, 0, 2), jnp.float32)
    pull_z = -0.5 * (ahead - behind)
    from_z = np.concatenate(
        [t.reshape(all_z, size_g, nz).transpose(1, 0, 2) for t in (table_z, pull_z)], axis=2
    )
    from_z = jnp.asarray(from_z, jnp.float32)
    keys_y = np.arange(all_y)
    table_y = jnp.asarray(hartley(keys_y, keys_y, all_y), jnp.float32)
    tables = jnp.asarray(decay_tables(all_x, all_y, all_z))
    flat_table = jnp.asarray(flat_mode_table(nx, all_x, all_y, all_z))

    scalar = pl.BlockSpec(memory_space=pltpu.SMEM)

    def call(kernel, inputs, out_shape, scratch=(), **more):
        specs = [scalar] + [pl.BlockSpec(memory_space=pltpu.VMEM)] * (len(inputs) - 1)
        return vmem_call(
            kernel, out_shape, in_specs=specs,
            scratch_shapes=[pltpu.VMEM(s, jnp.float32) for s in scratch], **more,
        )(*inputs)

    (spectral,) = call(along_z_kernel, (in_g, density, into_z), [(all_z, main)])
    spectral = lax.all_to_all(
        spectral.reshape(groups, kz, main), ("hy", "ga"), split_axis=0, concat_axis=0, tiled=True
    )

    cooled, xlo, xhi, ylo, yhi, zface = vmem_call(
        pack_kernel,
        [(nx, ny, nz)] + [(prim_n, ny, nz)] * 2 + [(prim_n, nx, nz)] * 2 + [(nx, ny, LANES)],
    )(density, velocity, pressure, species, newton_count)
    xbelow, xabove = shifted(xhi, "hx", 1), shifted(xlo, "hx", -1)
    ybelow, yabove = shifted(yhi, "hy", 1), shifted(ylo, "hy", -1)
    zbelow = shifted(zface, "ga", 1)
    zabove = zbelow if size_g == 2 else shifted(zface, "ga", -1)

    modes, sums = call(
        functools.partial(along_y_kernel, size_g, ny),
        (in_plane, spectral, table_y, tables),
        [(nx, kz, all_y), (2 * kz + nx, all_y)],
        [(nx * kz, all_y)],
    )
    others = [shifted(sums, "hx", s) for s in range(1, size_x)]
    (planes,) = call(
        functools.partial(along_x_kernel, size_x, size_g, ny),
        (in_plane, modes, sums, *others, table_y, tables, flat_table),
        [(groups, kz, width)],
        [(all_x, all_y), ((nx + 2) * kz, all_y), ((nx + 2) * kz, all_y)],
    )
    planes = lax.all_to_all(planes, ("hy", "ga"), split_axis=0, concat_axis=0, tiled=True)

    new_density, momentum, total_energy, species_mass = vmem_call(
        flux_kernel,
        [(nx, ny, nz), (3, nx, ny, nz), (nx, ny, nz), (species_n, nx, ny, nz)],
        scratch_shapes=[
            pltpu.VMEM((field_n, nx + 2, ny, nz), jnp.float32),
            pltpu.VMEM((2, field_n, nx, nz), jnp.float32),
        ],
    )(density, velocity, cooled, species, xbelow, xabove, ybelow, yabove, zbelow, zabove)

    potential, momentum, total_energy = call(
        gravity_kernel,
        (in_g, planes, from_z, density, velocity, momentum, total_energy),
        [(nx, ny, nz), (3, nx, ny, nz), (nx, ny, nz)],
        [(main, 2 * nz), (LANES, nz)],
    )
    return (new_density, momentum, total_energy, species_mass, potential)


def solution(mesh):
    cells = P("hx", "hy", "ga")
    fields = P(None, "hx", "hy", "ga")
    return jax.shard_map(
        local,
        mesh=mesh,
        in_specs=(cells, fields, cells, fields, cells),
        out_specs=(cells, fields, cells, fields, cells),
        check_vma=False,
    )
```

```python
import functools
import math

import jax
import jax.numpy as jnp
import numpy as np
from jax import lax
from jax.experimental import pallas as pl
from jax.experimental.pallas import tpu as pltpu
from jax.sharding import PartitionSpec as P


NEWTON = 4
gamma_gas = 5.0 / 3.0
time_step = 0.1
cool_rates = (2.0, 5.0, 9.0, 14.0, 20.0, 3.0, 7.0, 11.0, 29.0)
species_n = len(cool_rates)
prim_n = 5 + species_n
half_step = 0.5 * time_step
highest = lax.Precision.HIGHEST
LANES = 128
P_AT = prim_n
C_AT = prim_n + 1
V_AT = prim_n + 2
field_n = prim_n + 5
face_n = prim_n + 3
HIGH_FACE = 64


def fields_of(primitive):
    density, v0, v1, v2, pressure = primitive[:5]
    energy = pressure * (1.0 / (gamma_gas - 1.0)) + 0.5 * density * (v0 * v0 + v1 * v1 + v2 * v2)
    sound = jnp.sqrt(gamma_gas * pressure / density)
    return (
        [density, density * v0, density * v1, density * v2, energy]
        + list(primitive[5:])
        + [pressure, sound, v0, v1, v2]
    )


def cooled_plane(density, pressure, species, count):
    cooling = cool_rates[0] * species[0]
    for s in range(1, species_n):
        cooling = cooling + cool_rates[s] * species[s]
    stiffness = time_step * density * cooling
    initial = pressure / ((gamma_gas - 1.0) * density)
    energy = initial
    for step in range(NEWTON):
        above = 1.0 + energy
        residual = ((energy - initial) * above + stiffness * energy * energy) * above
        derivative = above * above + stiffness * energy * (energy + 2.0)
        energy = jnp.where(count > step, energy - residual / derivative, energy)
    return (gamma_gas - 1.0) * density * energy


def pack_kernel(den, vel, pre, spe, cnt, cooled, xlo, xhi, ylo, yhi, zface):
    nx, ny, nz = den.shape
    lane = lax.broadcasted_iota(jnp.int32, (ny, LANES), 1)

    def plane(x, _):
        density = den[x]
        species = [spe[s, x] for s in range(species_n)]
        pressure = cooled_plane(density, pre[x], species, cnt[x])
        cooled[x] = pressure
        primitive = [density, vel[0, x], vel[1, x], vel[2, x], pressure] + [density * s for s in species]
        for c in range(prim_n):
            ylo[c, pl.ds(x, 1), :] = primitive[c][0:1, :]
            yhi[c, pl.ds(x, 1), :] = primitive[c][ny - 1 : ny, :]

        @pl.when(x == 0)
        def _():
            for c in range(prim_n):
                xlo[c] = primitive[c]

        @pl.when(x == nx - 1)
        def _():
            for c in range(prim_n):
                xhi[c] = primitive[c]

        fields = fields_of(primitive)
        carried = fields[: C_AT + 1] + [fields[V_AT + 2]]
        packed = jnp.zeros((ny, LANES), jnp.float32)
        for c in range(face_n):
            first, last = carried[c][:, :LANES], carried[c][:, nz - LANES :]
            packed = jnp.where(lane == c, pltpu.roll(first, c, 1) if c else first, packed)
            packed = jnp.where(lane == HIGH_FACE + c, pltpu.roll(last, HIGH_FACE + c + 1, 1), packed)
        zface[x] = packed
        return 0

    lax.fori_loop(0, nx, plane, 0)


def flux_kernel(den, vel, cooled, spe, xbelow, xabove, ybelow, yabove, zbelow, zabove,
                new_density, momentum, energy, mass, ext, yedge):
    nx, ny, nz = den.shape
    row = lax.broadcasted_iota(jnp.int32, (ny, nz), 0)
    lane = lax.broadcasted_iota(jnp.int32, (ny, nz), 1)

    for at, face in ((0, xbelow), (nx + 1, xabove)):
        for f, value in enumerate(fields_of([face[c] for c in range(prim_n)])):
            ext[f, at] = value
    for side, face in enumerate((ybelow, yabove)):
        for f, value in enumerate(fields_of([face[c] for c in range(prim_n)])):
            yedge[side, f] = value

    def derive(x, _):
        density = den[x]
        primitive = [density, vel[0, x], vel[1, x], vel[2, x], cooled[x]]
        primitive += [density * spe[s, x] for s in range(species_n)]
        for f, value in enumerate(fields_of(primitive)):
            ext[f, x + 1] = value
        return 0

    lax.fori_loop(0, nx, derive, 0)

    def plane(x, _):
        from_below = zbelow[x]
        from_above = zabove[x]

        def beside(f, direction, up):
            if direction == 0:
                return ext[f, x + 2] if up else ext[f, x]
            here = ext[f, x + 1]
            if direction == 1:
                edge = yedge[1 if up else 0, f, pl.ds(x, 1), :]
                if up:
                    return jnp.where(row == ny - 1, edge, pltpu.roll(here, ny - 1, 0))
                return jnp.where(row == 0, edge, pltpu.roll(here, 1, 0))
            slot = f if f < V_AT else prim_n + 2
            if up:
                edge = pltpu.roll(from_above, LANES - 1 - slot, 1)
                return jnp.where(lane == nz - 1, edge, pltpu.roll(here, nz - 1, 1))
            edge = pltpu.roll(from_below, LANES - HIGH_FACE - slot, 1)
            return jnp.where(lane == 0, edge, pltpu.roll(here, 1, 1))

        sound = ext[C_AT, x + 1]
        centre = 1.0
        above, below, push, work = [], [], [], 0.0
        for d in range(3):
            speed = jnp.abs(ext[V_AT + d, x + 1]) + sound
            v_up, v_lo = beside(V_AT + d, d, True), beside(V_AT + d, d, False)
            p_up, p_lo = beside(P_AT, d, True), beside(P_AT, d, False)
            s_up = jnp.maximum(speed, jnp.abs(v_up) + beside(C_AT, d, True))
            s_lo = jnp.maximum(speed, jnp.abs(v_lo) + beside(C_AT, d, False))
            centre = centre - half_step * (s_up + s_lo)
            above.append(half_step * (s_up - v_up))
            below.append(half_step * (s_lo + v_lo))
            push.append(half_step * (p_lo - p_up))
            work = work + half_step * (p_lo * v_lo - p_up * v_up)

        def updated(f):
            total = centre * ext[f, x + 1]
            for d in range(3):
                total = total + above[d] * beside(f, d, True)
                total = total + below[d] * beside(f, d, False)
            return total

        new_density[x] = updated(0)
        for d in range(3):
            momentum[d, x] = updated(1 + d) + push[d]
        energy[x] = updated(4) + work
        for s in range(species_n):
            mass[s, x] = updated(5 + s)
        return 0

    lax.fori_loop(0, nx, plane, 0)


def vmem_call(kernel, out_shape, **more):
    return pl.pallas_call(
        kernel,
        out_shape=[jax.ShapeDtypeStruct(s, jnp.float32) for s in out_shape],
        **more,
    )


def shifted(value, axis, step):
    count = lax.axis_size(axis)
    return lax.ppermute(value, axis, [(i, (i + step) % count) for i in range(count)])


def hartley(rows, columns, length):
    angle = 2.0 * np.pi / length * (np.outer(rows, columns) % length)
    return np.cos(angle) + np.sin(angle)


def curvature(length):
    return 4.0 * np.sin(np.pi / length * np.arange(length)) ** 2


def decay_tables(nx, ny, nz):
    mu = curvature(nz)[:, None] + curvature(ny)[None, :]
    mu[0, 0] = 1.0
    root = np.sqrt(mu * (4.0 + mu))
    decay = 2.0 / (2.0 + mu + root)
    return np.stack([decay, 1.0 / (1.0 - decay**nx), -1.0 / (root * ny * nz)]).astype(np.float32)


def flat_mode_table(block, nx, ny, nz):
    rows = -(-(block + 2) // 8) * 8
    cell = np.arange(-1, rows - 1)[:, None]
    segment = np.arange(nx // block)[:, None]
    source = (np.arange(block)[None, :] - block * segment).reshape(1, -1)
    gap = (cell - source) % nx
    table = gap * (nx - gap) / (2.0 * nx) - (nx * nx - 1.0) / (12.0 * nx)
    return (table / (ny * nz)).astype(np.float32)


def along_z_kernel(part, den, table, out):
    nx, ny, nz = den.shape
    out[...] = lax.dot_general(
        table[part[0]], den[...].reshape(nx * ny, nz), (((1,), (1,)), ((), ())),
        precision=highest, preferred_element_type=jnp.float32,
    )


def segments(kz, width):
    return lax.broadcasted_iota(jnp.int32, (kz, LANES), 1) // width


def turned(value, lanes):
    lanes = lanes % LANES
    return pltpu.roll(value, lanes, 1) if lanes else value


def along_y_kernel(size_g, block, parts, lines, table_y, tables, modes, sums, grid_rows):
    _, kz, _ = lines.shape
    nx, _, ny = modes.shape
    width = block
    per = LANES // width
    place = segments(kz, width)
    for column in range(ny // LANES):
        for high in range(nx // per):
            source = []
            for s in range(per):
                first = (column * per + s) * size_g
                total = lines[first, :, high * LANES : (high + 1) * LANES]
                for g in range(1, size_g):
                    total = total + lines[first + g, :, high * LANES : (high + 1) * LANES]
                source.append(total)
            for low in range(per):
                line = turned(source[0], -low * width)
                for s in range(1, per):
                    line = jnp.where(place == s, turned(source[s], (s - low) * width), line)
                x = high * per + low
                grid_rows[x * kz : (x + 1) * kz, column * LANES : (column + 1) * LANES] = line
    spectrum = jnp.dot(
        grid_rows[...], table_y[...], precision=highest, preferred_element_type=jnp.float32
    )
    modes[...] = spectrum.reshape(nx, kz, ny)
    decay = tables[0, pl.ds(parts[0] * kz, kz), :]
    forward, backward = modes[0], modes[nx - 1]
    for x in range(1, nx):
        forward = forward * decay + modes[x]
        backward = backward * decay + modes[nx - 1 - x]
    sums[0:kz] = forward
    sums[kz : 2 * kz] = backward
    for x in range(nx):
        sums[2 * kz + x : 2 * kz + x + 1] = modes[x, 0:1, :]


def along_x_kernel(count, size_g, block, parts, modes, own, *rest):
    others = rest[: count - 1]
    table_y, tables, flat_table, out, gathered, potential, lines = rest[count - 1 :]
    nx, kz, ny = modes.shape
    width = block
    per = LANES // width
    for s in range(count):
        seen = own if s == 0 else others[s - 1]
        gathered[s * nx : (s + 1) * nx] = seen[2 * kz : 2 * kz + nx]
    flat = jnp.dot(
        flat_table[...], gathered[...], precision=highest, preferred_element_type=jnp.float32
    )
    for tile in range(0, kz, 8):
        rows = slice(tile, tile + 8)
        at = pl.ds(parts[0] * kz + tile, 8)
        decay, closing, scale = tables[0, at, :], tables[1, at, :], tables[2, at, :]
        far = decay
        for _ in range(int(math.log2(nx))):
            far = far * far
        left = own[tile : tile + 8]
        right = own[kz + tile : kz + tile + 8]
        for s in range(count - 1, 0, -1):
            left = left * far + others[s - 1][tile : tile + 8]
            right = right * far + others[count - s - 1][kz + tile : kz + tile + 8]
        left, right = left * closing, right * closing
        from_left = [left]
        for x in range(nx):
            from_left.append(from_left[-1] * decay + modes[x, rows])
        result = [None] * (nx + 2)
        result[nx + 1] = from_left[nx] * decay + right
        behind = right
        for x in range(nx - 1, -1, -1):
            result[x + 1] = behind * decay + from_left[x + 1]
            behind = behind * decay + modes[x, rows]
        result[0] = from_left[0] + behind * decay
        if tile == 0:
            first = lax.broadcasted_iota(jnp.int32, (8, ny), 0) + lax.broadcasted_iota(jnp.int32, (8, ny), 1)
            first = first + parts[0] == 0
        for x in range(nx + 2):
            value = result[x] * scale
            if tile == 0:
                value = jnp.where(first, flat[x : x + 1, :], value)
            potential[x * kz + tile : x * kz + tile + 8] = value
    lines[...] = jnp.dot(
        potential[...], table_y[...], precision=highest, preferred_element_type=jnp.float32
    )
    place = segments(kz, width)
    lane = lax.broadcasted_iota(jnp.int32, (kz, LANES), 1)

    def line(x, column):
        return lines[(x + 1) * kz : (x + 2) * kz, column * LANES : (column + 1) * LANES]

    for target in range(ny // width):
        column, s = target // per, target % per
        pieces = []
        for high in range(nx // per):
            piece = turned(line(high * per, column), -s * width)
            for low in range(1, per):
                piece = jnp.where(place == low, turned(line(high * per + low, column), (low - s) * width), piece)
            pieces.append(piece)
        edge = turned(line(-1, column), -s * width)
        edge = jnp.where(place == 1, turned(line(nx, column), (1 - s) * width), edge)
        for side, y in enumerate((target * width - 1, (target + 1) * width)):
            y = y % ny
            for x in range(nx):
                slot = 2 * width + side * nx + x
                edge = jnp.where(lane == slot, turned(line(x, y // LANES), slot - y % LANES), edge)
        pieces.append(edge)
        for g in range(size_g):
            for p, piece in enumerate(pieces):
                out[target * size_g + g, :, p * LANES : (p + 1) * LANES] = piece


def gravity_kernel(part, planes, table, den, vel, momentum_in, energy_in, potential, momentum, energy, solved, edges):
    nx, ny, nz = den.shape
    groups, kz, width = planes.shape
    main = nx * ny
    flat = planes[...].reshape(groups * kz, width)
    here = table[part[0]]
    contract = (((0,), (0,)), ((), ()))
    solved[...] = lax.dot_general(
        flat[:, :main], here, contract, precision=highest, preferred_element_type=jnp.float32
    )
    edges[...] = lax.dot_general(
        flat[:, main:], here[:, :nz], contract, precision=highest, preferred_element_type=jnp.float32
    )
    row = lax.broadcasted_iota(jnp.int32, (ny, nz), 0)
    for x in range(nx):
        value = solved[x * ny : (x + 1) * ny, :nz]
        potential[x] = value
        above = solved[(x + 1) * ny : (x + 2) * ny, :nz] if x < nx - 1 else edges[ny : 2 * ny]
        below = solved[(x - 1) * ny : x * ny, :nz] if x > 0 else edges[:ny]
        at = 2 * ny + x
        right = jnp.where(row == ny - 1, edges[at + nx : at + nx + 1], pltpu.roll(value, ny - 1, 0))
        left = jnp.where(row == 0, edges[at : at + 1], pltpu.roll(value, 1, 0))
        pull = time_step * den[x]
        kicks = [
            pull * (-0.5 * (above - below)),
            pull * (-0.5 * (right - left)),
            pull * solved[x * ny : (x + 1) * ny, nz:],
        ]
        work = energy_in[x]
        for d in range(3):
            momentum[d, x] = momentum_in[d, x] + kicks[d]
            work = work + kicks[d] * vel[d, x]
        energy[x] = work


def step(density, velocity, pressure, species, newton_count):
    size_x, size_y, size_g = (lax.axis_size(a) for a in ("hx", "hy", "ga"))
    nx, ny, nz = density.shape
    all_x, all_y, all_z = nx * size_x, ny * size_y, nz * size_g
    groups = size_y * size_g
    kz = all_z // groups
    in_g = lax.axis_index("ga").astype(jnp.int32).reshape(1)
    in_plane = (lax.axis_index("hy") * size_g + lax.axis_index("ga")).astype(jnp.int32).reshape(1)
    main = nx * ny
    width = main + LANES

    keys_z = np.arange(all_z)
    table_z = hartley(keys_z, keys_z, all_z)
    ahead = hartley(keys_z, keys_z + 1, all_z)
    behind = hartley(keys_z, keys_z - 1, all_z)
    into_z = jnp.asarray(table_z.reshape(all_z, size_g, nz).transpose(1, 0, 2), jnp.float32)
    pull_z = -0.5 * (ahead - behind)
    from_z = np.concatenate(
        [t.reshape(all_z, size_g, nz).transpose(1, 0, 2) for t in (table_z, pull_z)], axis=2
    )
    from_z = jnp.asarray(from_z, jnp.float32)
    keys_y = np.arange(all_y)
    table_y = jnp.asarray(hartley(keys_y, keys_y, all_y), jnp.float32)
    tables = jnp.asarray(decay_tables(all_x, all_y, all_z))
    flat_table = jnp.asarray(flat_mode_table(nx, all_x, all_y, all_z))

    scalar = pl.BlockSpec(memory_space=pltpu.SMEM)

    def call(kernel, inputs, out_shape, scratch=(), **more):
        specs = [scalar] + [pl.BlockSpec(memory_space=pltpu.VMEM)] * (len(inputs) - 1)
        return vmem_call(
            kernel, out_shape, in_specs=specs,
            scratch_shapes=[pltpu.VMEM(s, jnp.float32) for s in scratch], **more,
        )(*inputs)

    (spectral,) = call(along_z_kernel, (in_g, density, into_z), [(all_z, main)])
    spectral = lax.all_to_all(
        spectral.reshape(groups, kz, main), ("hy", "ga"), split_axis=0, concat_axis=0, tiled=True
    )

    cooled, xlo, xhi, ylo, yhi, zface = vmem_call(
        pack_kernel,
        [(nx, ny, nz)] + [(prim_n, ny, nz)] * 2 + [(prim_n, nx, nz)] * 2 + [(nx, ny, LANES)],
    )(density, velocity, pressure, species, newton_count)
    xbelow = shifted(xhi, "hx", 1)
    xabove = shifted(xlo, "hx", -1)
    ybelow = shifted(yhi, "hy", 1)
    yabove = shifted(ylo, "hy", -1)
    zbelow = shifted(zface, "ga", 1)
    zabove = zbelow if size_g == 2 else shifted(zface, "ga", -1)

    modes, sums = call(
        functools.partial(along_y_kernel, size_g, ny),
        (in_plane, spectral, table_y, tables),
        [(nx, kz, all_y), (2 * kz + nx, all_y)],
        [(nx * kz, all_y)],
    )
    others = [shifted(sums, "hx", s) for s in range(1, size_x)]
    (planes,) = call(
        functools.partial(along_x_kernel, size_x, size_g, ny),
        (in_plane, modes, sums, *others, table_y, tables, flat_table),
        [(groups, kz, width)],
        [(all_x, all_y), ((nx + 2) * kz, all_y), ((nx + 2) * kz, all_y)],
    )
    planes = lax.all_to_all(planes, ("hy", "ga"), split_axis=0, concat_axis=0, tiled=True)

    new_density, momentum, total_energy, species_mass = vmem_call(
        flux_kernel,
        [(nx, ny, nz), (3, nx, ny, nz), (nx, ny, nz), (species_n, nx, ny, nz)],
        scratch_shapes=[
            pltpu.VMEM((field_n, nx + 2, ny, nz), jnp.float32),
            pltpu.VMEM((2, field_n, nx, nz), jnp.float32),
        ],
    )(density, velocity, cooled, species, xbelow, xabove, ybelow, yabove, zbelow, zabove)

    potential, momentum, total_energy = call(
        gravity_kernel,
        (in_g, planes, from_z, density, velocity, momentum, total_energy),
        [(nx, ny, nz), (3, nx, ny, nz), (nx, ny, nz)],
        [(main, 2 * nz), (LANES, nz)],
    )
    return (new_density, momentum, total_energy, species_mass, potential)


def solution(mesh):
    cells = P("hx", "hy", "ga")
    fields = P(None, "hx", "hy", "ga")
    return jax.shard_map(
        step,
        mesh=mesh,
        in_specs=(cells, fields, cells, fields, cells),
        out_specs=(cells, fields, cells, fields, cells),
        check_vma=False,
    )
```

```python
import functools
import math

import jax
import jax.numpy as jnp
import numpy as np
from jax import lax
from jax.experimental import pallas as pl
from jax.experimental.pallas import tpu as pltpu
from jax.sharding import PartitionSpec as P


NEWTON = 4
gamma_gas = 5.0 / 3.0
time_step = 0.1
cool_rates = (2.0, 5.0, 9.0, 14.0, 20.0, 3.0, 7.0, 11.0, 29.0)
species_n = len(cool_rates)
prim_n = 5 + species_n
half_step = 0.5 * time_step
highest = lax.Precision.HIGHEST
LANES = 128
GRANT = 16 * 2**20
OUT_FIRST = "---"
OUT_PACK = "vhhhvvvv"
IN_Y = "-vv"
OUT_Y = "v-"
IN_OTHERS = "-"
IN_FLUX = "vHHHHHH"
IN_GRAVITY = "-vvvv"
P_AT = prim_n
C_AT = prim_n + 1
V_AT = prim_n + 2
field_n = prim_n + 5
face_n = prim_n + 3
HIGH_FACE = 64


def fields_of(primitive):
    density, v0, v1, v2, pressure = primitive[:5]
    energy = pressure * (1.0 / (gamma_gas - 1.0)) + 0.5 * density * (v0 * v0 + v1 * v1 + v2 * v2)
    sound = jnp.sqrt(gamma_gas * pressure / density)
    return (
        [density, density * v0, density * v1, density * v2, energy]
        + list(primitive[5:])
        + [pressure, sound, v0, v1, v2]
    )


def cooled_plane(density, pressure, species, count):
    cooling = cool_rates[0] * species[0]
    for s in range(1, species_n):
        cooling = cooling + cool_rates[s] * species[s]
    stiffness = time_step * density * cooling
    initial = pressure / ((gamma_gas - 1.0) * density)
    energy = initial
    for step in range(NEWTON):
        above = 1.0 + energy
        residual = ((energy - initial) * above + stiffness * energy * energy) * above
        derivative = above * above + stiffness * energy * (energy + 2.0)
        energy = jnp.where(count > step, energy - residual / derivative, energy)
    return (gamma_gas - 1.0) * density * energy


def copies_in(pairs, semaphores):
    started = []
    for n, (source, target) in enumerate(pairs):
        copy = pltpu.make_async_copy(source, target, semaphores.at[n])
        copy.start()
        started.append(copy)
    return started


def primitive_plane(x, den, vel, pre, spe, cnt):
    density = den[x]
    species = [spe[s, x] for s in range(species_n)]
    pressure = cooled_plane(density, pre[x], species, cnt[x])
    return [density, vel[0, x], vel[1, x], vel[2, x], pressure] + [density * s for s in species]


def first_kernel(part, den, vel, pre, spe, cnt, table, spectral, xlo, xhi,
                 den_in, vel_in, pre_in, spe_in, cnt_in, table_in, semaphores):
    nx, ny, nz = den.shape
    pairs = [(den, den_in), (table.at[part[0]], table_in)]
    for n, x in enumerate((0, nx - 1)):
        pairs += [(vel.at[:, x], vel_in.at[:, n]), (pre.at[x], pre_in.at[n])]
        pairs += [(spe.at[:, x], spe_in.at[:, n]), (cnt.at[x], cnt_in.at[n])]
    copies = copies_in(pairs, semaphores)
    copies[0].wait()
    copies[1].wait()
    spectral[...] = lax.dot_general(
        table_in[...], den_in[...].reshape(nx * ny, nz), (((1,), (1,)), ((), ())),
        precision=highest, preferred_element_type=jnp.float32,
    )
    for copy in copies[2:]:
        copy.wait()
    for n, (x, face) in enumerate(((0, xlo), (nx - 1, xhi))):
        species = [spe_in[s, n] for s in range(species_n)]
        density = den_in[x]
        pressure = cooled_plane(density, pre_in[n], species, cnt_in[n])
        for c, value in enumerate(
            [density, vel_in[0, n], vel_in[1, n], vel_in[2, n], pressure] + [density * s for s in species]
        ):
            face[c] = value


def pack_kernel(parts, den, vel, pre, spe, cnt, table_y, tables, from_z, flat_table,
                fields, ylo, yhi, zface, own_y, own_decay, own_z, own_flat,
                den_in, vel_in, pre_in, spe_in, cnt_in, plane_semaphores, semaphores):
    nx, ny, nz = den.shape
    kz = own_decay.shape[1]
    lane = lax.broadcasted_iota(jnp.int32, (ny, LANES), 1)
    arguments = ((den, den_in), (vel, vel_in), (pre, pre_in), (spe, spe_in), (cnt, cnt_in))

    def plane_of(ref, x):
        return ref.at[:, x] if len(ref.shape) == 4 else ref.at[x]

    def plane_copies(x):
        return [
            pltpu.make_async_copy(plane_of(a, x), plane_of(b, x), plane_semaphores.at[n, x])
            for n, (a, b) in enumerate(arguments)
        ]

    for x in range(nx):
        for copy in plane_copies(x):
            copy.start()
    later = copies_in(
        [
            (table_y, own_y),
            (tables.at[:, pl.ds(parts[1] * kz, kz), :], own_decay),
            (from_z.at[parts[0]], own_z),
            (flat_table, own_flat),
        ],
        semaphores,
    )

    def plane(x, _):
        for copy in plane_copies(x):
            copy.wait()
        primitive = primitive_plane(x, den_in, vel_in, pre_in, spe_in, cnt_in)
        for c in range(prim_n):
            ylo[c, pl.ds(x, 1), :] = primitive[c][0:1, :]
            yhi[c, pl.ds(x, 1), :] = primitive[c][ny - 1 : ny, :]
        derived = fields_of(primitive)
        for f in range(field_n):
            fields[f, x] = derived[f]
        carried = derived[: C_AT + 1] + [derived[V_AT + 2]]
        packed = jnp.zeros((ny, LANES), jnp.float32)
        for c in range(face_n):
            first, last = carried[c][:, :LANES], carried[c][:, nz - LANES :]
            packed = jnp.where(lane == c, pltpu.roll(first, c, 1) if c else first, packed)
            packed = jnp.where(lane == HIGH_FACE + c, pltpu.roll(last, HIGH_FACE + c + 1, 1), packed)
        zface[x] = packed
        return 0

    lax.fori_loop(0, nx, plane, 0)
    for copy in later:
        copy.wait()


def flux_kernel(fields, xbelow, xabove, ybelow, yabove, zbelow, zabove,
                new_density, momentum, energy, mass, xedge, yedge):
    _, nx, ny, nz = fields.shape
    row = lax.broadcasted_iota(jnp.int32, (ny, nz), 0)
    lane = lax.broadcasted_iota(jnp.int32, (ny, nz), 1)

    for side, face in enumerate((xbelow, xabove)):
        for f, value in enumerate(fields_of([face[c] for c in range(prim_n)])):
            xedge[side, f] = value
    for side, face in enumerate((ybelow, yabove)):
        for f, value in enumerate(fields_of([face[c] for c in range(prim_n)])):
            yedge[side, f] = value

    def plane(x, lower, upper):
        from_below = zbelow[x]
        from_above = zabove[x]

        def beside(f, direction, up):
            if direction == 0:
                return upper(f) if up else lower(f)
            here = fields[f, x]
            if direction == 1:
                edge = yedge[1 if up else 0, f, pl.ds(x, 1), :]
                if up:
                    return jnp.where(row == ny - 1, edge, pltpu.roll(here, ny - 1, 0))
                return jnp.where(row == 0, edge, pltpu.roll(here, 1, 0))
            slot = f if f < V_AT else prim_n + 2
            if up:
                edge = pltpu.roll(from_above, LANES - 1 - slot, 1)
                return jnp.where(lane == nz - 1, edge, pltpu.roll(here, nz - 1, 1))
            edge = pltpu.roll(from_below, LANES - HIGH_FACE - slot, 1)
            return jnp.where(lane == 0, edge, pltpu.roll(here, 1, 1))

        sound = fields[C_AT, x]
        centre = 1.0
        above, below, push, work = [], [], [], 0.0
        for d in range(3):
            speed = jnp.abs(fields[V_AT + d, x]) + sound
            v_up, v_lo = beside(V_AT + d, d, True), beside(V_AT + d, d, False)
            p_up, p_lo = beside(P_AT, d, True), beside(P_AT, d, False)
            s_up = jnp.maximum(speed, jnp.abs(v_up) + beside(C_AT, d, True))
            s_lo = jnp.maximum(speed, jnp.abs(v_lo) + beside(C_AT, d, False))
            centre = centre - half_step * (s_up + s_lo)
            above.append(half_step * (s_up - v_up))
            below.append(half_step * (s_lo + v_lo))
            push.append(half_step * (p_lo - p_up))
            work = work + half_step * (p_lo * v_lo - p_up * v_up)

        def updated(f):
            total = centre * fields[f, x]
            for d in range(3):
                total = total + above[d] * beside(f, d, True)
                total = total + below[d] * beside(f, d, False)
            return total

        new_density[x] = updated(0)
        for d in range(3):
            momentum[d, x] = updated(1 + d) + push[d]
        energy[x] = updated(4) + work
        for s in range(species_n):
            mass[s, x] = updated(5 + s)

    def inner(x, _):
        plane(x, lambda f: fields[f, x - 1], lambda f: fields[f, x + 1])
        return 0

    plane(0, lambda f: xedge[0, f], lambda f: fields[f, 1])
    lax.fori_loop(1, nx - 1, inner, 0)
    plane(nx - 1, lambda f: fields[f, nx - 2], lambda f: xedge[1, f])


SPACES = {"h": pltpu.HBM, "v": pltpu.VMEM}


def placed_call(kernel, inputs, in_spaces, outputs, out_spaces, scratch):
    specs, operands = [], []
    for value, space in zip(inputs, in_spaces, strict=True):
        if space == "s":
            specs.append(pl.BlockSpec(memory_space=pltpu.SMEM))
        else:
            specs.append(pl.BlockSpec(memory_space=pl.ANY if space == "h" else pltpu.VMEM))
            if space != "-":
                value = pltpu.with_memory_space_constraint(value, SPACES[space.lower()])
        operands.append(value)
    shapes = [
        jax.ShapeDtypeStruct(shape, jnp.float32) if space == "-" else SPACES[space](shape, jnp.float32)
        for shape, space in zip(outputs, out_spaces, strict=True)
    ]
    return pl.pallas_call(
        kernel,
        out_shape=shapes,
        in_specs=specs,
        out_specs=[pl.BlockSpec(memory_space=pltpu.VMEM)] * len(shapes),
        scratch_shapes=scratch,
        compiler_params=pltpu.CompilerParams(vmem_limit_bytes=GRANT),
    )(*operands)


def shifted(value, axis, step):
    count = lax.axis_size(axis)
    return lax.ppermute(value, axis, [(i, (i + step) % count) for i in range(count)])


def hartley(rows, columns, length):
    angle = 2.0 * np.pi / length * (np.outer(rows, columns) % length)
    return np.cos(angle) + np.sin(angle)


def curvature(length):
    return 4.0 * np.sin(np.pi / length * np.arange(length)) ** 2


def decay_tables(nx, ny, nz):
    mu = curvature(nz)[:, None] + curvature(ny)[None, :]
    mu[0, 0] = 1.0
    root = np.sqrt(mu * (4.0 + mu))
    decay = 2.0 / (2.0 + mu + root)
    return np.stack([decay, 1.0 / (1.0 - decay**nx), -1.0 / (root * ny * nz)]).astype(np.float32)


def flat_mode_table(block, nx, ny, nz):
    rows = -(-(block + 2) // 8) * 8
    cell = np.arange(-1, rows - 1)[:, None]
    segment = np.arange(nx // block)[:, None]
    source = (np.arange(block)[None, :] - block * segment).reshape(1, -1)
    gap = (cell - source) % nx
    table = gap * (nx - gap) / (2.0 * nx) - (nx * nx - 1.0) / (12.0 * nx)
    return (table / (ny * nz)).astype(np.float32)


def segments(kz, width):
    return lax.broadcasted_iota(jnp.int32, (kz, LANES), 1) // width


def turned(value, lanes):
    lanes = lanes % LANES
    return pltpu.roll(value, lanes, 1) if lanes else value


def along_y_kernel(size_g, block, lines, table_y, tables, modes, sums, grid_rows):
    _, kz, _ = lines.shape
    nx, _, ny = modes.shape
    width = block
    per = LANES // width
    place = segments(kz, width)
    for column in range(ny // LANES):
        for high in range(nx // per):
            source = []
            for s in range(per):
                first = (column * per + s) * size_g
                total = lines[first, :, high * LANES : (high + 1) * LANES]
                for g in range(1, size_g):
                    total = total + lines[first + g, :, high * LANES : (high + 1) * LANES]
                source.append(total)
            for low in range(per):
                line = turned(source[0], -low * width)
                for s in range(1, per):
                    line = jnp.where(place == s, turned(source[s], (s - low) * width), line)
                x = high * per + low
                grid_rows[x * kz : (x + 1) * kz, column * LANES : (column + 1) * LANES] = line
    spectrum = jnp.dot(
        grid_rows[...], table_y[...], precision=highest, preferred_element_type=jnp.float32
    )
    modes[...] = spectrum.reshape(nx, kz, ny)
    decay = tables[0]
    forward, backward = modes[0], modes[nx - 1]
    for x in range(1, nx):
        forward = forward * decay + modes[x]
        backward = backward * decay + modes[nx - 1 - x]
    sums[0:kz] = forward
    sums[kz : 2 * kz] = backward
    for x in range(nx):
        sums[2 * kz + x : 2 * kz + x + 1] = modes[x, 0:1, :]


def along_x_kernel(count, size_g, block, parts, modes, own, *rest):
    others = rest[: count - 1]
    table_y, tables, flat_table, out, gathered, potential, lines = rest[count - 1 :]
    nx, kz, ny = modes.shape
    width = block
    per = LANES // width
    for s in range(count):
        seen = own if s == 0 else others[s - 1]
        gathered[s * nx : (s + 1) * nx] = seen[2 * kz : 2 * kz + nx]
    flat = jnp.dot(
        flat_table[...], gathered[...], precision=highest, preferred_element_type=jnp.float32
    )
    for tile in range(0, kz, 8):
        rows = slice(tile, tile + 8)
        decay, closing, scale = tables[0, rows], tables[1, rows], tables[2, rows]
        far = decay
        for _ in range(int(math.log2(nx))):
            far = far * far
        left = own[tile : tile + 8]
        right = own[kz + tile : kz + tile + 8]
        for s in range(count - 1, 0, -1):
            left = left * far + others[s - 1][tile : tile + 8]
            right = right * far + others[count - s - 1][kz + tile : kz + tile + 8]
        left, right = left * closing, right * closing
        from_left = [left]
        for x in range(nx):
            from_left.append(from_left[-1] * decay + modes[x, rows])
        result = [None] * (nx + 2)
        result[nx + 1] = from_left[nx] * decay + right
        behind = right
        for x in range(nx - 1, -1, -1):
            result[x + 1] = behind * decay + from_left[x + 1]
            behind = behind * decay + modes[x, rows]
        result[0] = from_left[0] + behind * decay
        if tile == 0:
            first = lax.broadcasted_iota(jnp.int32, (8, ny), 0) + lax.broadcasted_iota(jnp.int32, (8, ny), 1)
            first = first + parts[1] == 0
        for x in range(nx + 2):
            value = result[x] * scale
            if tile == 0:
                value = jnp.where(first, flat[x : x + 1, :], value)
            potential[x * kz + tile : x * kz + tile + 8] = value
    lines[...] = jnp.dot(
        potential[...], table_y[...], precision=highest, preferred_element_type=jnp.float32
    )
    place = segments(kz, width)
    lane = lax.broadcasted_iota(jnp.int32, (kz, LANES), 1)

    def line(x, column):
        return lines[(x + 1) * kz : (x + 2) * kz, column * LANES : (column + 1) * LANES]

    for target in range(ny // width):
        column, s = target // per, target % per
        pieces = []
        for high in range(nx // per):
            piece = turned(line(high * per, column), -s * width)
            for low in range(1, per):
                piece = jnp.where(place == low, turned(line(high * per + low, column), (low - s) * width), piece)
            pieces.append(piece)
        edge = turned(line(-1, column), -s * width)
        edge = jnp.where(place == 1, turned(line(nx, column), (1 - s) * width), edge)
        for side, y in enumerate((target * width - 1, (target + 1) * width)):
            y = y % ny
            for x in range(nx):
                slot = 2 * width + side * nx + x
                edge = jnp.where(lane == slot, turned(line(x, y // LANES), slot - y % LANES), edge)
        pieces.append(edge)
        for g in range(size_g):
            for p, piece in enumerate(pieces):
                out[target * size_g + g, :, p * LANES : (p + 1) * LANES] = piece


def gravity_kernel(planes, table, fields, momentum_in, energy_in, potential, momentum, energy, solved, edges):
    _, nx, ny, nz = fields.shape
    groups, kz, width = planes.shape
    main = nx * ny
    flat = planes[...].reshape(groups * kz, width)
    here = table[...]
    contract = (((0,), (0,)), ((), ()))
    solved[...] = lax.dot_general(
        flat[:, :main], here, contract, precision=highest, preferred_element_type=jnp.float32
    )
    edges[...] = lax.dot_general(
        flat[:, main:], here[:, :nz], contract, precision=highest, preferred_element_type=jnp.float32
    )
    row = lax.broadcasted_iota(jnp.int32, (ny, nz), 0)
    for x in range(nx):
        value = solved[x * ny : (x + 1) * ny, :nz]
        potential[x] = value
        above = solved[(x + 1) * ny : (x + 2) * ny, :nz] if x < nx - 1 else edges[ny : 2 * ny]
        below = solved[(x - 1) * ny : x * ny, :nz] if x > 0 else edges[:ny]
        at = 2 * ny + x
        right = jnp.where(row == ny - 1, edges[at + nx : at + nx + 1], pltpu.roll(value, ny - 1, 0))
        left = jnp.where(row == 0, edges[at : at + 1], pltpu.roll(value, 1, 0))
        pull = time_step * fields[0, x]
        kicks = [
            pull * (-0.5 * (above - below)),
            pull * (-0.5 * (right - left)),
            pull * solved[x * ny : (x + 1) * ny, nz:],
        ]
        work = energy_in[x]
        for d in range(3):
            momentum[d, x] = momentum_in[d, x] + kicks[d]
            work = work + kicks[d] * fields[V_AT + d, x]
        energy[x] = work


def step(density, velocity, pressure, species, newton_count):
    size_x, size_y, size_g = (lax.axis_size(a) for a in ("hx", "hy", "ga"))
    nx, ny, nz = density.shape
    all_x, all_y, all_z = nx * size_x, ny * size_y, nz * size_g
    groups = size_y * size_g
    kz = all_z // groups
    rank_g = lax.axis_index("ga").astype(jnp.int32)
    rank = lax.axis_index("hy").astype(jnp.int32) * size_g + rank_g
    parts = jnp.stack([rank_g, rank])
    main = nx * ny
    width = main + LANES

    keys_z = np.arange(all_z)
    table_z = hartley(keys_z, keys_z, all_z)
    ahead = hartley(keys_z, keys_z + 1, all_z)
    behind = hartley(keys_z, keys_z - 1, all_z)
    into_z = jnp.asarray(table_z.reshape(all_z, size_g, nz).transpose(1, 0, 2), jnp.float32)
    pull_z = -0.5 * (ahead - behind)
    from_z = np.concatenate(
        [t.reshape(all_z, size_g, nz).transpose(1, 0, 2) for t in (table_z, pull_z)], axis=2
    )
    from_z = jnp.asarray(from_z, jnp.float32)
    keys_y = np.arange(all_y)
    table_y = jnp.asarray(hartley(keys_y, keys_y, all_y), jnp.float32)
    tables = jnp.asarray(decay_tables(all_x, all_y, all_z))
    flat_table = jnp.asarray(flat_mode_table(nx, all_x, all_y, all_z))

    floats = functools.partial(pltpu.VMEM, dtype=jnp.float32)
    gas = (density, velocity, pressure, species, newton_count)

    spectral, xlo, xhi = placed_call(
        first_kernel,
        (parts, *gas, into_z),
        "shhhhhh",
        [(all_z, main), (prim_n, ny, nz), (prim_n, ny, nz)],
        OUT_FIRST,
        [
            floats((nx, ny, nz)),
            floats((3, 2, ny, nz)),
            floats((2, ny, nz)),
            floats((species_n, 2, ny, nz)),
            pltpu.VMEM((2, ny, nz), jnp.int32),
            floats((all_z, nz)),
            pltpu.SemaphoreType.DMA((10,)),
        ],
    )
    xbelow = shifted(xhi, "hx", 1)
    xabove = shifted(xlo, "hx", -1)
    spectral = lax.all_to_all(
        spectral.reshape(groups, kz, main), ("hy", "ga"), split_axis=0, concat_axis=0, tiled=True
    )
    fields, ylo, yhi, zface, own_y, own_decay, own_z, own_flat = placed_call(
        pack_kernel,
        (parts, *gas, table_y, tables, from_z, flat_table),
        "shhhhhhhhh",
        [(field_n, nx, ny, nz)] + [(prim_n, nx, nz)] * 2 + [(nx, ny, LANES)]
        + [table_y.shape, (3, kz, all_y), from_z.shape[1:], flat_table.shape],
        OUT_PACK,
        [
            floats((nx, ny, nz)),
            floats((3, nx, ny, nz)),
            floats((nx, ny, nz)),
            floats((species_n, nx, ny, nz)),
            pltpu.VMEM((nx, ny, nz), jnp.int32),
            pltpu.SemaphoreType.DMA((5, nx)),
            pltpu.SemaphoreType.DMA((4,)),
        ],
    )
    modes, sums = placed_call(
        functools.partial(along_y_kernel, size_g, ny),
        (spectral, own_y, own_decay),
        IN_Y,
        [(nx, kz, all_y), (2 * kz + nx, all_y)],
        OUT_Y,
        [floats((nx * kz, all_y))],
    )
    others = [shifted(sums, "hx", s) for s in range(1, size_x)]
    ybelow = shifted(yhi, "hy", 1)
    yabove = shifted(ylo, "hy", -1)
    zbelow = shifted(zface, "ga", 1)
    zabove = zbelow if size_g == 2 else shifted(zface, "ga", -1)
    (planes,) = placed_call(
        functools.partial(along_x_kernel, size_x, size_g, ny),
        (parts, modes, sums, *others, own_y, own_decay, own_flat),
        "sv-" + IN_OTHERS * (size_x - 1) + "vvv",
        [(groups, kz, width)],
        "-",
        [floats((all_x, all_y)), floats(((nx + 2) * kz, all_y)), floats(((nx + 2) * kz, all_y))],
    )
    planes = lax.all_to_all(planes, ("hy", "ga"), split_axis=0, concat_axis=0, tiled=True)
    new_density, momentum, total_energy, species_mass = placed_call(
        flux_kernel,
        (fields, xbelow, xabove, ybelow, yabove, zbelow, zabove),
        IN_FLUX,
        [(nx, ny, nz), (3, nx, ny, nz), (nx, ny, nz), (species_n, nx, ny, nz)],
        "-vv-",
        [floats((2, field_n, ny, nz)), floats((2, field_n, nx, nz))],
    )
    potential, momentum, total_energy = placed_call(
        gravity_kernel,
        (planes, own_z, fields, momentum, total_energy),
        IN_GRAVITY,
        [(nx, ny, nz), (3, nx, ny, nz), (nx, ny, nz)],
        "---",
        [floats((main, 2 * nz)), floats((LANES, nz))],
    )
    return (new_density, momentum, total_energy, species_mass, potential)


def solution(mesh):
    cells = P("hx", "hy", "ga")
    fields = P(None, "hx", "hy", "ga")
    return jax.shard_map(
        step,
        mesh=mesh,
        in_specs=(cells, fields, cells, fields, cells),
        out_specs=(cells, fields, cells, fields, cells),
        check_vma=False,
    )
```

```python
import functools
import math

import jax
import jax.numpy as jnp
import numpy as np
from jax import lax
from jax.experimental import pallas as pl
from jax.experimental.pallas import tpu as pltpu
from jax.sharding import PartitionSpec as P


NEWTON = 4
gamma_gas = 5.0 / 3.0
time_step = 0.1
cool_rates = (2.0, 5.0, 9.0, 14.0, 20.0, 3.0, 7.0, 11.0, 29.0)
species_n = len(cool_rates)
prim_n = 5 + species_n
half_step = 0.5 * time_step
highest = lax.Precision.HIGHEST
LANES = 128
GRANT = 16 * 2**20
OUT_FIRST = "vvvvvvvv"
OUT_PACK = "vvvhhhvvv"
IN_Y = "-vv"
OUT_Y = "v-"
IN_OTHERS = "-"
OUT_X = "h"
IN_FLUX = "svvvvvhhvvvvh"
IN_GRAVITY = "-vvvv"
P_AT = 4
C_AT = prim_n
face_n = prim_n + 3
HIGH_FACE = 64


def sound_speed(density, pressure):
    return jnp.sqrt(gamma_gas * pressure / density)


def conserved(kept):
    density, v0, v1, v2, pressure = kept[:5]
    energy = pressure * (1.0 / (gamma_gas - 1.0)) + 0.5 * density * (v0 * v0 + v1 * v1 + v2 * v2)
    return [density, density * v0, density * v1, density * v2, energy] + list(kept[5:prim_n])


def cooled_plane(density, pressure, species, count):
    cooling = cool_rates[0] * species[0]
    for s in range(1, species_n):
        cooling = cooling + cool_rates[s] * species[s]
    stiffness = time_step * density * cooling
    initial = pressure / ((gamma_gas - 1.0) * density)
    energy = initial
    for step in range(NEWTON):
        above = 1.0 + energy
        residual = ((energy - initial) * above + stiffness * energy * energy) * above
        derivative = above * above + stiffness * energy * (energy + 2.0)
        energy = jnp.where(count > step, energy - residual / derivative, energy)
    return (gamma_gas - 1.0) * density * energy


def copies_in(pairs, semaphores):
    started = []
    for n, (source, target) in enumerate(pairs):
        copy = pltpu.make_async_copy(source, target, semaphores.at[n])
        copy.start()
        started.append(copy)
    return started


def primitive_plane(x, den, vel, pre, spe, cnt):
    density = den[x]
    species = [spe[s, x] for s in range(species_n)]
    pressure = cooled_plane(density, pre[x], species, cnt[x])
    return [density, vel[0, x], vel[1, x], vel[2, x], pressure] + [density * s for s in species]


def first_kernel(part, den, vel, pre, spe, cnt, table, spectral, xlo, xhi,
                 den_in, vel_in, pre_in, spe_in, cnt_in, table_in, semaphores):
    nx, ny, nz = den.shape
    copies = copies_in(
        [(den, den_in), (table.at[part[0]], table_in), (pre, pre_in), (cnt, cnt_in), (spe, spe_in), (vel, vel_in)],
        semaphores,
    )
    copies[0].wait()
    copies[1].wait()
    spectral[...] = lax.dot_general(
        table_in[...], den_in[...].reshape(nx * ny, nz), (((1,), (1,)), ((), ())),
        precision=highest, preferred_element_type=jnp.float32,
    )
    for copy in copies[2:]:
        copy.wait()
    for x, face in ((0, xlo), (nx - 1, xhi)):
        for c, value in enumerate(primitive_plane(x, den_in, vel_in, pre_in, spe_in, cnt_in)):
            face[c] = value


def pack_kernel(parts, den, vel, pre, spe, cnt, table_y, tables, flat_table,
                cooled, mass, sound, ylo, yhi, zface, own_y, own_decay, own_flat, semaphores):
    nx, ny, nz = den.shape
    kz = own_decay.shape[1]
    lane = lax.broadcasted_iota(jnp.int32, (ny, LANES), 1)
    later = copies_in(
        [
            (table_y, own_y),
            (tables.at[:, pl.ds(parts[1] * kz, kz), :], own_decay),
            (flat_table, own_flat),
        ],
        semaphores,
    )

    def plane(x, _):
        primitive = primitive_plane(x, den, vel, pre, spe, cnt)
        for c in range(prim_n):
            ylo[c, pl.ds(x, 1), :] = primitive[c][0:1, :]
            yhi[c, pl.ds(x, 1), :] = primitive[c][ny - 1 : ny, :]
        kept = primitive + [sound_speed(primitive[0], primitive[P_AT])]
        cooled[x] = kept[P_AT]
        for s in range(species_n):
            mass[s, x] = kept[P_AT + 1 + s]
        sound[x] = kept[C_AT]
        carried = conserved(kept) + [kept[P_AT], kept[C_AT], kept[3]]
        packed = jnp.zeros((ny, LANES), jnp.float32)
        for c in range(face_n):
            first, last = carried[c][:, :LANES], carried[c][:, nz - LANES :]
            packed = jnp.where(lane == c, pltpu.roll(first, c, 1) if c else first, packed)
            packed = jnp.where(lane == HIGH_FACE + c, pltpu.roll(last, HIGH_FACE + c + 1, 1), packed)
        zface[x] = packed
        return 0

    lax.fori_loop(0, nx, plane, 0)
    for copy in later:
        copy.wait()


def flux_kernel(parts, den, vel, cooled, dense, speed_of, xbelow, xabove, ybelow, yabove, zbelow, zabove, from_z,
                new_density, carried, mass, own_z, xfaces, yedge, semaphores):
    nx, ny, nz = den.shape
    row = lax.broadcasted_iota(jnp.int32, (ny, nz), 0)
    lane = lax.broadcasted_iota(jnp.int32, (ny, nz), 1)
    copies = copies_in(
        [(xbelow, xfaces.at[0]), (xabove, xfaces.at[1]), (from_z.at[parts[0]], own_z)], semaphores
    )

    def with_flow(kept):
        return conserved(kept) + [kept[P_AT], kept[C_AT], kept[1], kept[2], kept[3]]

    def stored(x):
        kept = [den[x], vel[0, x], vel[1, x], vel[2, x], cooled[x]]
        return with_flow(kept + [dense[s, x] for s in range(species_n)] + [speed_of[x]])

    def faced(face):
        kept = [face[c] for c in range(prim_n)]
        return with_flow(kept + [sound_speed(kept[0], kept[P_AT])])

    flow_p, flow_c, flow_v = prim_n, prim_n + 1, prim_n + 2
    for side, face in enumerate((ybelow, yabove)):
        for f, value in enumerate(faced(face)):
            yedge[side, f] = value

    def plane(x, lower, upper):
        from_below = zbelow[x]
        from_above = zabove[x]
        centre = stored(x)

        def beside(f, direction, up):
            if direction == 0:
                return upper[f] if up else lower[f]
            here = centre[f]
            if direction == 1:
                edge = yedge[1 if up else 0, f, pl.ds(x, 1), :]
                if up:
                    return jnp.where(row == ny - 1, edge, pltpu.roll(here, ny - 1, 0))
                return jnp.where(row == 0, edge, pltpu.roll(here, 1, 0))
            slot = f if f < flow_v else flow_v
            if up:
                edge = pltpu.roll(from_above, LANES - 1 - slot, 1)
                return jnp.where(lane == nz - 1, edge, pltpu.roll(here, nz - 1, 1))
            edge = pltpu.roll(from_below, LANES - HIGH_FACE - slot, 1)
            return jnp.where(lane == 0, edge, pltpu.roll(here, 1, 1))

        stay = 1.0
        above, below, push, work = [], [], [], 0.0
        for d in range(3):
            speed = jnp.abs(centre[flow_v + d]) + centre[flow_c]
            v_up, v_lo = beside(flow_v + d, d, True), beside(flow_v + d, d, False)
            p_up, p_lo = beside(flow_p, d, True), beside(flow_p, d, False)
            s_up = jnp.maximum(speed, jnp.abs(v_up) + beside(flow_c, d, True))
            s_lo = jnp.maximum(speed, jnp.abs(v_lo) + beside(flow_c, d, False))
            stay = stay - half_step * (s_up + s_lo)
            above.append(half_step * (s_up - v_up))
            below.append(half_step * (s_lo + v_lo))
            push.append(half_step * (p_lo - p_up))
            work = work + half_step * (p_lo * v_lo - p_up * v_up)

        def updated(f):
            total = stay * centre[f]
            for d in range(3):
                total = total + above[d] * beside(f, d, True)
                total = total + below[d] * beside(f, d, False)
            return total

        new_density[x] = updated(0)
        for d in range(3):
            carried[d, x] = updated(1 + d) + push[d]
        carried[3, x] = updated(4) + work
        for s in range(species_n):
            mass[s, x] = updated(5 + s)

    def inner(x, _):
        plane(x, stored(x - 1), stored(x + 1))
        return 0

    lax.fori_loop(1, nx - 1, inner, 0)
    copies[0].wait()
    plane(0, faced(xfaces.at[0]), stored(1))
    copies[1].wait()
    plane(nx - 1, stored(nx - 2), faced(xfaces.at[1]))
    copies[2].wait()


SPACES = {"h": pltpu.HBM, "v": pltpu.VMEM}


def placed_call(kernel, inputs, in_spaces, outputs, out_spaces, scratch, aliases={}):
    specs, operands = [], []
    for value, space in zip(inputs, in_spaces, strict=True):
        if space == "s":
            specs.append(pl.BlockSpec(memory_space=pltpu.SMEM))
        else:
            specs.append(pl.BlockSpec(memory_space=pl.ANY if space == "h" else pltpu.VMEM))
            if space != "-":
                value = pltpu.with_memory_space_constraint(value, SPACES[space.lower()])
        operands.append(value)
    shapes = []
    for shape, space in zip(outputs, out_spaces, strict=True):
        shape, kind = (shape, jnp.float32) if isinstance(shape, tuple) else (shape.shape, shape.dtype)
        shapes.append(jax.ShapeDtypeStruct(shape, kind) if space == "-" else SPACES[space](shape, kind))
    return pl.pallas_call(
        kernel,
        out_shape=shapes,
        in_specs=specs,
        out_specs=[pl.BlockSpec(memory_space=pltpu.VMEM)] * len(shapes),
        scratch_shapes=scratch,
        input_output_aliases=aliases,
        compiler_params=pltpu.CompilerParams(vmem_limit_bytes=GRANT),
    )(*operands)


def shifted(value, axis, step):
    count = lax.axis_size(axis)
    return lax.ppermute(value, axis, [(i, (i + step) % count) for i in range(count)])


def hartley(rows, columns, length):
    angle = 2.0 * np.pi / length * (np.outer(rows, columns) % length)
    return np.cos(angle) + np.sin(angle)


def curvature(length):
    return 4.0 * np.sin(np.pi / length * np.arange(length)) ** 2


def decay_tables(nx, ny, nz):
    mu = curvature(nz)[:, None] + curvature(ny)[None, :]
    mu[0, 0] = 1.0
    root = np.sqrt(mu * (4.0 + mu))
    decay = 2.0 / (2.0 + mu + root)
    return np.stack([decay, 1.0 / (1.0 - decay**nx), -1.0 / (root * ny * nz)]).astype(np.float32)


def flat_mode_table(block, nx, ny, nz):
    rows = -(-(block + 2) // 8) * 8
    cell = np.arange(-1, rows - 1)[:, None]
    segment = np.arange(nx // block)[:, None]
    source = (np.arange(block)[None, :] - block * segment).reshape(1, -1)
    gap = (cell - source) % nx
    table = gap * (nx - gap) / (2.0 * nx) - (nx * nx - 1.0) / (12.0 * nx)
    return (table / (ny * nz)).astype(np.float32)


def segments(kz, width):
    return lax.broadcasted_iota(jnp.int32, (kz, LANES), 1) // width


def turned(value, lanes):
    lanes = lanes % LANES
    return pltpu.roll(value, lanes, 1) if lanes else value


def along_y_kernel(size_g, block, lines, table_y, tables, modes, sums, grid_rows):
    _, kz, _ = lines.shape
    nx, _, ny = modes.shape
    width = block
    per = LANES // width
    place = segments(kz, width)
    for column in range(ny // LANES):
        for high in range(nx // per):
            source = []
            for s in range(per):
                first = (column * per + s) * size_g
                total = lines[first, :, high * LANES : (high + 1) * LANES]
                for g in range(1, size_g):
                    total = total + lines[first + g, :, high * LANES : (high + 1) * LANES]
                source.append(total)
            for low in range(per):
                line = turned(source[0], -low * width)
                for s in range(1, per):
                    line = jnp.where(place == s, turned(source[s], (s - low) * width), line)
                x = high * per + low
                grid_rows[x * kz : (x + 1) * kz, column * LANES : (column + 1) * LANES] = line
    spectrum = jnp.dot(
        grid_rows[...], table_y[...], precision=highest, preferred_element_type=jnp.float32
    )
    modes[...] = spectrum.reshape(nx, kz, ny)
    decay = tables[0]
    forward, backward = modes[0], modes[nx - 1]
    for x in range(1, nx):
        forward = forward * decay + modes[x]
        backward = backward * decay + modes[nx - 1 - x]
    sums[0:kz] = forward
    sums[kz : 2 * kz] = backward
    for x in range(nx):
        sums[2 * kz + x : 2 * kz + x + 1] = modes[x, 0:1, :]


def along_x_kernel(count, size_g, block, parts, modes, own, *rest):
    others = rest[: count - 1]
    table_y, tables, flat_table, out, gathered, potential, lines = rest[count - 1 :]
    nx, kz, ny = modes.shape
    width = block
    per = LANES // width
    for s in range(count):
        seen = own if s == 0 else others[s - 1]
        gathered[s * nx : (s + 1) * nx] = seen[2 * kz : 2 * kz + nx]
    flat = jnp.dot(
        flat_table[...], gathered[...], precision=highest, preferred_element_type=jnp.float32
    )
    for tile in range(0, kz, 8):
        rows = slice(tile, tile + 8)
        decay, closing, scale = tables[0, rows], tables[1, rows], tables[2, rows]
        far = decay
        for _ in range(int(math.log2(nx))):
            far = far * far
        left = own[tile : tile + 8]
        right = own[kz + tile : kz + tile + 8]
        for s in range(count - 1, 0, -1):
            left = left * far + others[s - 1][tile : tile + 8]
            right = right * far + others[count - s - 1][kz + tile : kz + tile + 8]
        left, right = left * closing, right * closing
        from_left = [left]
        for x in range(nx):
            from_left.append(from_left[-1] * decay + modes[x, rows])
        result = [None] * (nx + 2)
        result[nx + 1] = from_left[nx] * decay + right
        behind = right
        for x in range(nx - 1, -1, -1):
            result[x + 1] = behind * decay + from_left[x + 1]
            behind = behind * decay + modes[x, rows]
        result[0] = from_left[0] + behind * decay
        if tile == 0:
            first = lax.broadcasted_iota(jnp.int32, (8, ny), 0) + lax.broadcasted_iota(jnp.int32, (8, ny), 1)
            first = first + parts[1] == 0
        for x in range(nx + 2):
            value = result[x] * scale
            if tile == 0:
                value = jnp.where(first, flat[x : x + 1, :], value)
            potential[x * kz + tile : x * kz + tile + 8] = value
    lines[...] = jnp.dot(
        potential[...], table_y[...], precision=highest, preferred_element_type=jnp.float32
    )
    place = segments(kz, width)
    lane = lax.broadcasted_iota(jnp.int32, (kz, LANES), 1)

    def line(x, column):
        return lines[(x + 1) * kz : (x + 2) * kz, column * LANES : (column + 1) * LANES]

    for target in range(ny // width):
        column, s = target // per, target % per
        pieces = []
        for high in range(nx // per):
            piece = turned(line(high * per, column), -s * width)
            for low in range(1, per):
                piece = jnp.where(place == low, turned(line(high * per + low, column), (low - s) * width), piece)
            pieces.append(piece)
        edge = turned(line(-1, column), -s * width)
        edge = jnp.where(place == 1, turned(line(nx, column), (1 - s) * width), edge)
        for side, y in enumerate((target * width - 1, (target + 1) * width)):
            y = y % ny
            for x in range(nx):
                slot = 2 * width + side * nx + x
                edge = jnp.where(lane == slot, turned(line(x, y // LANES), slot - y % LANES), edge)
        pieces.append(edge)
        for g in range(size_g):
            for p, piece in enumerate(pieces):
                out[target * size_g + g, :, p * LANES : (p + 1) * LANES] = piece


def gravity_kernel(planes, table, den, vel, carried, potential, momentum, energy, solved, edges):
    nx, ny, nz = den.shape
    groups, kz, width = planes.shape
    main = nx * ny
    flat = planes[...].reshape(groups * kz, width)
    here = table[...]
    contract = (((0,), (0,)), ((), ()))
    solved[...] = lax.dot_general(
        flat[:, :main], here, contract, precision=highest, preferred_element_type=jnp.float32
    )
    edges[...] = lax.dot_general(
        flat[:, main:], here[:, :nz], contract, precision=highest, preferred_element_type=jnp.float32
    )
    row = lax.broadcasted_iota(jnp.int32, (ny, nz), 0)
    for x in range(nx):
        value = solved[x * ny : (x + 1) * ny, :nz]
        potential[x] = value
        above = solved[(x + 1) * ny : (x + 2) * ny, :nz] if x < nx - 1 else edges[ny : 2 * ny]
        below = solved[(x - 1) * ny : x * ny, :nz] if x > 0 else edges[:ny]
        at = 2 * ny + x
        right = jnp.where(row == ny - 1, edges[at + nx : at + nx + 1], pltpu.roll(value, ny - 1, 0))
        left = jnp.where(row == 0, edges[at : at + 1], pltpu.roll(value, 1, 0))
        pull = time_step * den[x]
        kicks = [
            pull * (-0.5 * (above - below)),
            pull * (-0.5 * (right - left)),
            pull * solved[x * ny : (x + 1) * ny, nz:],
        ]
        work = carried[3, x]
        for d in range(3):
            momentum[d, x] = carried[d, x] + kicks[d]
            work = work + kicks[d] * vel[d, x]
        energy[x] = work


def step(density, velocity, pressure, species, newton_count):
    size_x, size_y, size_g = (lax.axis_size(a) for a in ("hx", "hy", "ga"))
    nx, ny, nz = density.shape
    all_x, all_y, all_z = nx * size_x, ny * size_y, nz * size_g
    groups = size_y * size_g
    kz = all_z // groups
    rank_g = lax.axis_index("ga").astype(jnp.int32)
    rank = lax.axis_index("hy").astype(jnp.int32) * size_g + rank_g
    parts = jnp.stack([rank_g, rank])
    main = nx * ny
    width = main + LANES

    keys_z = np.arange(all_z)
    table_z = hartley(keys_z, keys_z, all_z)
    ahead = hartley(keys_z, keys_z + 1, all_z)
    behind = hartley(keys_z, keys_z - 1, all_z)
    into_z = jnp.asarray(table_z.reshape(all_z, size_g, nz).transpose(1, 0, 2), jnp.float32)
    pull_z = -0.5 * (ahead - behind)
    from_z = np.concatenate(
        [t.reshape(all_z, size_g, nz).transpose(1, 0, 2) for t in (table_z, pull_z)], axis=2
    )
    from_z = jnp.asarray(from_z, jnp.float32)
    keys_y = np.arange(all_y)
    table_y = jnp.asarray(hartley(keys_y, keys_y, all_y), jnp.float32)
    tables = jnp.asarray(decay_tables(all_x, all_y, all_z))
    flat_table = jnp.asarray(flat_mode_table(nx, all_x, all_y, all_z))

    floats = functools.partial(pltpu.VMEM, dtype=jnp.float32)

    spectral, xlo, xhi, den, vel, pre, spe, cnt = placed_call(
        first_kernel,
        (parts, density, velocity, pressure, species, newton_count, into_z),
        "shhhhhh",
        [(all_z, main), (prim_n, ny, nz), (prim_n, ny, nz)]
        + [density.shape, velocity.shape, pressure.shape, species.shape, newton_count],
        OUT_FIRST,
        [floats((all_z, nz)), pltpu.SemaphoreType.DMA((6,))],
    )
    xbelow = shifted(xhi, "hx", 1)
    xabove = shifted(xlo, "hx", -1)
    spectral = lax.all_to_all(spectral.reshape(groups, kz, main), ("hy", "ga"), split_axis=0, concat_axis=0, tiled=True)
    cooled, dense, sound, ylo, yhi, zface, own_y, own_decay, own_flat = placed_call(
        pack_kernel,
        (parts, den, vel, pre, spe, cnt, table_y, tables, flat_table),
        "svvvvvhhh",
        [pre.shape, spe.shape, pre.shape] + [(prim_n, nx, nz)] * 2 + [(nx, ny, LANES)]
        + [table_y.shape, (3, kz, all_y), flat_table.shape],
        OUT_PACK,
        [pltpu.SemaphoreType.DMA((3,))],
        {3: 0, 4: 1},
    )
    modes, sums = placed_call(
        functools.partial(along_y_kernel, size_g, ny),
        (spectral, own_y, own_decay),
        IN_Y,
        [(nx, kz, all_y), (2 * kz + nx, all_y)],
        OUT_Y,
        [floats((nx * kz, all_y))],
    )
    others = [shifted(sums, "hx", s) for s in range(1, size_x)]
    ybelow = shifted(yhi, "hy", 1)
    yabove = shifted(ylo, "hy", -1)
    zbelow = shifted(zface, "ga", 1)
    zabove = zbelow if size_g == 2 else shifted(zface, "ga", -1)
    (planes,) = placed_call(
        functools.partial(along_x_kernel, size_x, size_g, ny),
        (parts, modes, sums, *others, own_y, own_decay, own_flat),
        "sv-" + IN_OTHERS * (size_x - 1) + "vvv",
        [(groups, kz, width)],
        OUT_X,
        [
            floats((all_x, all_y)),
            floats(((nx + 2) * kz, all_y)),
            floats(((nx + 2) * kz, all_y)),
        ],
    )
    planes = lax.all_to_all(planes, ("hy", "ga"), split_axis=0, concat_axis=0, tiled=True)
    new_density, carried, species_mass, own_z = placed_call(
        flux_kernel,
        (parts, den, vel, cooled, dense, sound, xbelow, xabove, ybelow, yabove, zbelow, zabove, from_z),
        IN_FLUX,
        [(nx, ny, nz), (4, nx, ny, nz), (species_n, nx, ny, nz), from_z.shape[1:]],
        "-v-v",
        [floats((2, prim_n, ny, nz)), floats((2, prim_n + 5, nx, nz)), pltpu.SemaphoreType.DMA((3,))],
    )
    potential, momentum, total_energy = placed_call(
        gravity_kernel,
        (planes, own_z, den, vel, carried),
        IN_GRAVITY,
        [(nx, ny, nz), (3, nx, ny, nz), (nx, ny, nz)],
        "---",
        [floats((main, 2 * nz)), floats((LANES, nz))],
    )
    return (new_density, momentum, total_energy, species_mass, potential)


def solution(mesh):
    cells = P("hx", "hy", "ga")
    fields = P(None, "hx", "hy", "ga")
    return jax.shard_map(
        step,
        mesh=mesh,
        in_specs=(cells, fields, cells, fields, cells),
        out_specs=(cells, fields, cells, fields, cells),
        check_vma=False,
    )
```

```python
import functools
import math

import jax
import jax.numpy as jnp
import numpy as np
from jax import lax
from jax.experimental import pallas as pl
from jax.experimental.pallas import tpu as pltpu
from jax.sharding import PartitionSpec as P


NEWTON = 4
gamma_gas = 5.0 / 3.0
time_step = 0.1
cool_rates = (2.0, 5.0, 9.0, 14.0, 20.0, 3.0, 7.0, 11.0, 29.0)
species_n = len(cool_rates)
prim_n = 5 + species_n
half_step = 0.5 * time_step
highest = lax.Precision.HIGHEST
LANES = 128
GRANT = 16 * 2**20
OUT_FIRST = "vvvvvv"
OUT_PACK = "vvvhhhhhvvv"
IN_Y = "-vv"
OUT_Y = "v-"
IN_OTHERS = "-"
OUT_X = "h"
IN_FLUX = "vvvvvvvvvh"
OUT_FLUX = "xxvvv"
IN_RIM = "vvvvvvhhhh"
OUT_RIM = "xxv"
IN_GRAVITY = "-vvvvv"
P_AT = 4
C_AT = prim_n
face_n = prim_n + 3


def sound_speed(density, pressure):
    return jnp.sqrt(gamma_gas * pressure / density)


def conserved(kept):
    density, v0, v1, v2, pressure = kept[:5]
    energy = pressure * (1.0 / (gamma_gas - 1.0)) + 0.5 * density * (v0 * v0 + v1 * v1 + v2 * v2)
    return [density, density * v0, density * v1, density * v2, energy] + list(kept[5:prim_n])


def cooled_plane(density, pressure, species, count):
    cooling = cool_rates[0] * species[0]
    for s in range(1, species_n):
        cooling = cooling + cool_rates[s] * species[s]
    stiffness = time_step * density * cooling
    initial = pressure / ((gamma_gas - 1.0) * density)
    energy = initial
    for step in range(NEWTON):
        above = 1.0 + energy
        residual = ((energy - initial) * above + stiffness * energy * energy) * above
        derivative = above * above + stiffness * energy * (energy + 2.0)
        energy = jnp.where(count > step, energy - residual / derivative, energy)
    return (gamma_gas - 1.0) * density * energy


def copies_in(pairs, semaphores):
    started = []
    for n, (source, target) in enumerate(pairs):
        copy = pltpu.make_async_copy(source, target, semaphores.at[n])
        copy.start()
        started.append(copy)
    return started


def primitive_plane(x, den, vel, pre, spe, cnt):
    density = den[x]
    species = [spe[s, x] for s in range(species_n)]
    pressure = cooled_plane(density, pre[x], species, cnt[x])
    return [density, vel[0, x], vel[1, x], vel[2, x], pressure] + [density * s for s in species]


def place_in_plane():
    in_g = lax.axis_index("ga")
    return in_g, lax.axis_index("hy") * lax.axis_size("ga") + in_g


def first_kernel(den, vel, pre, spe, cnt, table, spectral,
                 den_in, vel_in, pre_in, spe_in, cnt_in, table_in, semaphores):
    nx, ny, nz = den.shape
    in_g, _ = place_in_plane()
    needed = copies_in([(den, den_in), (table.at[in_g], table_in)], semaphores.at[0])
    copies = copies_in([(pre, pre_in), (cnt, cnt_in), (spe, spe_in), (vel, vel_in)], semaphores.at[1])
    for copy in needed:
        copy.wait()
    spectral[...] = lax.dot_general(
        table_in[...], den_in[...].reshape(nx * ny, nz), (((1,), (1,)), ((), ())),
        precision=highest, preferred_element_type=jnp.float32,
    )
    for copy in copies:
        copy.wait()


def pack_kernel(den, vel, pre, spe, cnt, table_y, tables, flat_table,
                cooled, mass, sound, xfirst, xlast, ylo, yhi, zface, own_y, own_decay, own_flat, semaphores):
    nx, ny, nz = den.shape
    kz = own_decay.shape[1]
    _, place = place_in_plane()
    lane = lax.broadcasted_iota(jnp.int32, (ny, LANES), 1)
    later = copies_in(
        [
            (table_y, own_y),
            (tables.at[:, pl.ds(place * kz, kz), :], own_decay),
            (flat_table, own_flat),
        ],
        semaphores,
    )

    second, _ = face_roles("hx")

    def plane(x, _):
        primitive = primitive_plane(x, den, vel, pre, spe, cnt)
        for at, face in (((nx - 1) * (1 - second), xfirst), ((nx - 1) * second, xlast)):

            @pl.when(x == at)
            def _():
                for c in range(prim_n):
                    face[c] = primitive[c]

        kept = primitive + [sound_speed(primitive[0], primitive[P_AT])]
        cooled[x] = kept[P_AT]
        for s in range(species_n):
            mass[s, x] = kept[P_AT + 1 + s]
        sound[x] = kept[C_AT]
        carried = conserved(kept) + [kept[P_AT], kept[C_AT], kept[3]]
        packed = jnp.zeros((ny, LANES), jnp.float32)
        for c in range(face_n):
            packed = jnp.where(lane // 2 == c, pltpu.roll(carried[c], 2 * c + 1, 1), packed)
        zface[x] = packed
        return 0

    lax.fori_loop(0, nx, plane, 0)
    kept = [den] + [vel.at[d] for d in range(3)] + [cooled] + [mass.at[s] for s in range(species_n)]
    for c in range(prim_n):
        rows = kept[c].reshape(nx * ny, nz)
        ylo[c] = rows[pl.ds(0, nx, stride=ny), :]
        yhi[c] = rows[pl.ds(ny - 1, nx, stride=ny), :]
    for copy in later:
        copy.wait()


flow_p, flow_c, flow_v = prim_n, prim_n + 1, prim_n + 2
flow_n = prim_n + 5


def with_flow(kept):
    return conserved(kept) + [kept[P_AT], kept[C_AT], kept[1], kept[2], kept[3]]


def faced(face):
    kept = [face[c] for c in range(prim_n)]
    return with_flow(kept + [sound_speed(kept[0], kept[P_AT])])


def stored(x, den, vel, cooled, dense, speed_of):
    kept = [den[x], vel[0, x], vel[1, x], vel[2, x], cooled[x]]
    return with_flow(kept + [dense[s, x] for s in range(species_n)] + [speed_of[x]])


def flux_kernel(den, vel, cooled, dense, speed_of, ybelow, yabove, zbelow, zabove, from_z,
                new_density, mass, carried, rim, own_z, ready, yedge, out_semaphores, semaphores):
    nx, ny, nz = den.shape
    row = lax.broadcasted_iota(jnp.int32, (ny, nz), 0)
    lane = lax.broadcasted_iota(jnp.int32, (ny, nz), 1)
    copies = copies_in([(from_z.at[place_in_plane()[0]], own_z)], semaphores)
    state = (den, vel, cooled, dense, speed_of)
    for side, face in enumerate((ybelow, yabove)):
        for f, value in enumerate(faced(face)):
            yedge[side, f] = value

    def plane(x, lower, upper):
        from_below = zbelow[x]
        from_above = zabove[x]
        centre = stored(x, *state)

        def beside(f, direction, up):
            if direction == 0:
                return upper[f] if up else lower[f]
            here = centre[f]
            if direction == 1:
                edge = yedge[1 if up else 0, f, pl.ds(x, 1), :]
                if up:
                    return jnp.where(row == ny - 1, edge, pltpu.roll(here, ny - 1, 0))
                return jnp.where(row == 0, edge, pltpu.roll(here, 1, 0))
            slot = f if f < flow_v else flow_v
            if up:
                edge = pltpu.roll(from_above, (LANES - 2 - 2 * slot) % LANES, 1)
                return jnp.where(lane == nz - 1, edge, pltpu.roll(here, nz - 1, 1))
            edge = pltpu.roll(from_below, (LANES - 2 * slot) % LANES, 1)
            return jnp.where(lane == 0, edge, pltpu.roll(here, 1, 1))

        stay, work = 1.0, 0.0
        weights, push = [], []
        for d in range(3):
            speed = jnp.abs(centre[flow_v + d]) + centre[flow_c]
            pushed = 0.0
            for up in (False, True):
                if d == 0 and (upper if up else lower) is None:
                    continue
                sign = -1.0 if up else 1.0
                v, p = beside(flow_v + d, d, up), beside(flow_p, d, up)
                signal = jnp.maximum(speed, jnp.abs(v) + beside(flow_c, d, up))
                stay = stay - half_step * signal
                weights.append((d, up, half_step * (signal + sign * v)))
                pushed = pushed + sign * half_step * p
                work = work + sign * half_step * (p * v)
            push.append(pushed)

        def updated(f):
            total = stay * centre[f]
            for d, up, weight in weights:
                total = total + weight * beside(f, d, up)
            return total

        result = [updated(f) for f in range(prim_n)]
        for d in range(3):
            result[1 + d] = result[1 + d] + push[d]
        result[4] = result[4] + work
        return result

    def leave(x):
        return [
            pltpu.make_async_copy(ready.at[0, x - 1], new_density.at[x], out_semaphores.at[0, x - 1]),
            pltpu.make_async_copy(
                ready.at[pl.ds(1, species_n), x - 1], mass.at[:, x], out_semaphores.at[1, x - 1]
            ),
        ]

    def inner(x, _):
        result = plane(x, stored(x - 1, *state), stored(x + 1, *state))
        ready[0, x - 1] = result[0]
        for d in range(4):
            carried[d, x] = result[1 + d]
        for s in range(species_n):
            ready[1 + s, x - 1] = result[5 + s]
        for copy in leave(x):
            copy.start()
        return 0

    def left(x, _):
        for copy in leave(x):
            copy.wait()
        return 0

    lax.fori_loop(1, nx - 1, inner, 0)
    for f, value in enumerate(plane(0, None, stored(1, *state))):
        rim[f, 0] = value
    for f, value in enumerate(plane(nx - 1, stored(nx - 2, *state), None)):
        rim[f, 1] = value
    for copy in copies:
        copy.wait()
    lax.fori_loop(1, nx - 1, left, 0)


def rim_kernel(den, vel, cooled, dense, speed_of, rim, xfirst, xlast, density_in, mass_in,
               new_density, mass, carried_rim, xfaces, ready, semaphores, out_semaphores):
    nx, _, _ = den.shape
    _, slot = face_roles("hx")
    copies = copies_in([(xfirst, xfaces.at[slot]), (xlast, xfaces.at[1 - slot])], semaphores)
    for copy in copies:
        copy.wait()
    leaving = []
    for n, (x, sign) in enumerate(((0, 1.0), (nx - 1, -1.0))):
        centre = stored(x, den, vel, cooled, dense, speed_of)
        other = faced(xfaces.at[n])
        v, p = other[flow_v], other[flow_p]
        signal = jnp.maximum(jnp.abs(centre[flow_v]) + centre[flow_c], jnp.abs(v) + other[flow_c])
        lost, weight = half_step * signal, half_step * (signal + sign * v)
        result = [rim[f, n] - lost * centre[f] + weight * other[f] for f in range(prim_n)]
        result[1] = result[1] + sign * half_step * p
        result[4] = result[4] + sign * half_step * (p * v)
        ready[0, n] = result[0]
        for d in range(4):
            carried_rim[d, n] = result[1 + d]
        for s in range(species_n):
            ready[1 + s, n] = result[5 + s]
        leaving += copies_in(
            [(ready.at[0, n], new_density.at[x]), (ready.at[pl.ds(1, species_n), n], mass.at[:, x])],
            out_semaphores.at[n],
        )
    for copy in leaving:
        copy.wait()


SPACES = {"h": pltpu.HBM, "v": pltpu.VMEM, "x": pltpu.HBM}


def placed_call(kernel, inputs, in_spaces, outputs, out_spaces, scratch, aliases={}):
    specs, operands = [], []
    for value, space in zip(inputs, in_spaces, strict=True):
        specs.append(pl.BlockSpec(memory_space=pl.ANY if space == "h" else pltpu.VMEM))
        if space != "-":
            value = pltpu.with_memory_space_constraint(value, SPACES[space])
        operands.append(value)
    shapes = []
    for shape, space in zip(outputs, out_spaces, strict=True):
        shape, kind = (shape, jnp.float32) if isinstance(shape, tuple) else (shape.shape, shape.dtype)
        shapes.append(jax.ShapeDtypeStruct(shape, kind) if space == "-" else SPACES[space](shape, kind))
    return pl.pallas_call(
        kernel,
        out_shape=shapes,
        in_specs=specs,
        out_specs=[pl.BlockSpec(memory_space=pl.ANY if space == "x" else pltpu.VMEM) for space in out_spaces],
        scratch_shapes=scratch,
        input_output_aliases=aliases,
        compiler_params=pltpu.CompilerParams(vmem_limit_bytes=GRANT),
    )(*operands)


def exchanged(value, axis, step):
    count = lax.axis_size(axis)
    return lax.ppermute(value, axis, [(i, partner(i, step, count)) for i in range(count)])


def partner(index, step, count):
    return index ^ step if count & (count - 1) == 0 else (index + step) % count


def source_of(index, step, count):
    return index ^ step if count & (count - 1) == 0 else lax.rem(index + count - step, count)


def face_roles(axis):
    if lax.axis_size(axis) % 2:
        return 0, 0
    second = lax.rem(lax.axis_index(axis), 2)
    return second, 1 - second


def faced_pairs(value, axis, first_round):
    count = lax.axis_size(axis)
    if count % 2:
        return shifted(value, axis, 1 if first_round else -1)
    start = 0 if first_round else 1
    pairs = [((start + i) % count, (start + i + 1) % count) for i in range(0, count, 2)]
    return lax.ppermute(value, axis, pairs + [(b, a) for a, b in pairs])


def shifted(value, axis, step):
    count = lax.axis_size(axis)
    return lax.ppermute(value, axis, [(i, (i + step) % count) for i in range(count)])


def hartley(rows, columns, length):
    angle = 2.0 * np.pi / length * (np.outer(rows, columns) % length)
    return np.cos(angle) + np.sin(angle)


def curvature(length):
    return 4.0 * np.sin(np.pi / length * np.arange(length)) ** 2


def decay_tables(nx, ny, nz):
    mu = curvature(nz)[:, None] + curvature(ny)[None, :]
    mu[0, 0] = 1.0
    root = np.sqrt(mu * (4.0 + mu))
    decay = 2.0 / (2.0 + mu + root)
    return np.stack([decay, 1.0 / (1.0 - decay**nx), -1.0 / (root * ny * nz)]).astype(np.float32)


def flat_mode_table(block, nx, ny, nz):
    rows = -(-(block + 2) // 8) * 8
    cell = np.arange(-1, rows - 1)[:, None]
    segment = np.arange(nx // block)[:, None]
    source = (np.arange(block)[None, :] - block * segment).reshape(1, -1)
    gap = (cell - source) % nx
    table = gap * (nx - gap) / (2.0 * nx) - (nx * nx - 1.0) / (12.0 * nx)
    return (table / (ny * nz)).astype(np.float32)


def segments(kz, width):
    return lax.broadcasted_iota(jnp.int32, (kz, LANES), 1) // width


def turned(value, lanes):
    lanes = lanes % LANES
    return pltpu.roll(value, lanes, 1) if lanes else value


def along_y_kernel(size_g, block, lines, table_y, tables, modes, sums, grid_rows):
    _, kz, _ = lines.shape
    nx, _, ny = modes.shape
    width = block
    per = LANES // width
    place = segments(kz, width)
    for column in range(ny // LANES):
        for high in range(nx // per):
            source = []
            for s in range(per):
                first = (column * per + s) * size_g
                total = lines[first, :, high * LANES : (high + 1) * LANES]
                for g in range(1, size_g):
                    total = total + lines[first + g, :, high * LANES : (high + 1) * LANES]
                source.append(total)
            for low in range(per):
                line = turned(source[0], -low * width)
                for s in range(1, per):
                    line = jnp.where(place == s, turned(source[s], (s - low) * width), line)
                x = high * per + low
                grid_rows[x * kz : (x + 1) * kz, column * LANES : (column + 1) * LANES] = line
    spectrum = jnp.dot(
        grid_rows[...], table_y[...], precision=highest, preferred_element_type=jnp.float32
    )
    modes[...] = spectrum.reshape(nx, kz, ny)
    decay = tables[0]
    forward, backward = modes[0], modes[nx - 1]
    for x in range(1, nx):
        forward = forward * decay + modes[x]
        backward = backward * decay + modes[nx - 1 - x]
    sums[0:kz] = forward
    sums[kz : 2 * kz] = backward
    for x in range(nx):
        sums[2 * kz + x : 2 * kz + x + 1] = modes[x, 0:1, :]


def along_x_kernel(count, size_g, block, modes, own, *rest):
    others = rest[: count - 1]
    table_y, tables, flat_table, out, everyone, gathered, potential, lines = rest[count - 1 :]
    me = lax.axis_index("hx")
    everyone[me] = own[...]
    for step in range(1, count):
        everyone[source_of(me, step, count)] = others[step - 1][...]

    def seen(distance):
        return everyone.at[lax.rem(me + count - distance, count)]

    nx, kz, ny = modes.shape
    width = block
    per = LANES // width
    for s in range(count):
        gathered[s * nx : (s + 1) * nx] = seen(s)[2 * kz : 2 * kz + nx]
    flat = jnp.dot(
        flat_table[...], gathered[...], precision=highest, preferred_element_type=jnp.float32
    )
    for tile in range(0, kz, 8):
        rows = slice(tile, tile + 8)
        decay, closing, scale = tables[0, rows], tables[1, rows], tables[2, rows]
        far = decay
        for _ in range(int(math.log2(nx))):
            far = far * far
        left = own[tile : tile + 8]
        right = own[kz + tile : kz + tile + 8]
        for s in range(count - 1, 0, -1):
            left = left * far + seen(s)[tile : tile + 8]
            right = right * far + seen(count - s)[kz + tile : kz + tile + 8]
        left, right = left * closing, right * closing
        from_left = [left]
        for x in range(nx):
            from_left.append(from_left[-1] * decay + modes[x, rows])
        result = [None] * (nx + 2)
        result[nx + 1] = from_left[nx] * decay + right
        behind = right
        for x in range(nx - 1, -1, -1):
            result[x + 1] = behind * decay + from_left[x + 1]
            behind = behind * decay + modes[x, rows]
        result[0] = from_left[0] + behind * decay
        if tile == 0:
            first = lax.broadcasted_iota(jnp.int32, (8, ny), 0) + lax.broadcasted_iota(jnp.int32, (8, ny), 1)
            first = first + place_in_plane()[1] == 0
        for x in range(nx + 2):
            value = result[x] * scale
            if tile == 0:
                value = jnp.where(first, flat[x : x + 1, :], value)
            potential[x * kz + tile : x * kz + tile + 8] = value
    lines[...] = jnp.dot(
        potential[...], table_y[...], precision=highest, preferred_element_type=jnp.float32
    )
    place = segments(kz, width)
    lane = lax.broadcasted_iota(jnp.int32, (kz, LANES), 1)

    def line(x, column):
        return lines[(x + 1) * kz : (x + 2) * kz, column * LANES : (column + 1) * LANES]

    for target in range(ny // width):
        column, s = target // per, target % per
        pieces = []
        for high in range(nx // per):
            piece = turned(line(high * per, column), -s * width)
            for low in range(1, per):
                piece = jnp.where(place == low, turned(line(high * per + low, column), (low - s) * width), piece)
            pieces.append(piece)
        edge = turned(line(-1, column), -s * width)
        edge = jnp.where(place == 1, turned(line(nx, column), (1 - s) * width), edge)
        for side, y in enumerate((target * width - 1, (target + 1) * width)):
            y = y % ny
            for x in range(nx):
                slot = 2 * width + side * nx + x
                edge = jnp.where(lane == slot, turned(line(x, y // LANES), slot - y % LANES), edge)
        pieces.append(edge)
        for g in range(size_g):
            for p, piece in enumerate(pieces):
                out[target * size_g + g, :, p * LANES : (p + 1) * LANES] = piece


def gravity_kernel(planes, table, den, vel, carried, carried_rim, potential, momentum, energy, solved, edges):
    nx, ny, nz = den.shape
    groups, kz, width = planes.shape
    main = nx * ny
    flat = planes[...].reshape(groups * kz, width)
    here = table[...]
    contract = (((0,), (0,)), ((), ()))
    solved[...] = lax.dot_general(
        flat[:, :main], here, contract, precision=highest, preferred_element_type=jnp.float32
    )
    edges[...] = lax.dot_general(
        flat[:, main:], here[:, :nz], contract, precision=highest, preferred_element_type=jnp.float32
    )
    row = lax.broadcasted_iota(jnp.int32, (ny, nz), 0)
    for x in range(nx):
        value = solved[x * ny : (x + 1) * ny, :nz]
        potential[x] = value
        above = solved[(x + 1) * ny : (x + 2) * ny, :nz] if x < nx - 1 else edges[ny : 2 * ny]
        below = solved[(x - 1) * ny : x * ny, :nz] if x > 0 else edges[:ny]
        at = 2 * ny + x
        right = jnp.where(row == ny - 1, edges[at + nx : at + nx + 1], pltpu.roll(value, ny - 1, 0))
        left = jnp.where(row == 0, edges[at : at + 1], pltpu.roll(value, 1, 0))
        pull = time_step * den[x]
        kicks = [
            pull * (-0.5 * (above - below)),
            pull * (-0.5 * (right - left)),
            pull * solved[x * ny : (x + 1) * ny, nz:],
        ]
        before = [carried_rim[d, x // (nx - 1)] if x in (0, nx - 1) else carried[d, x] for d in range(4)]
        work = before[3]
        for d in range(3):
            momentum[d, x] = before[d] + kicks[d]
            work = work + kicks[d] * vel[d, x]
        energy[x] = work


def step(density, velocity, pressure, species, newton_count):
    size_x, size_y, size_g = (lax.axis_size(a) for a in ("hx", "hy", "ga"))
    nx, ny, nz = density.shape
    all_x, all_y, all_z = nx * size_x, ny * size_y, nz * size_g
    groups = size_y * size_g
    kz = all_z // groups
    main = nx * ny
    width = main + LANES

    keys_z = np.arange(all_z)
    table_z = hartley(keys_z, keys_z, all_z)
    ahead = hartley(keys_z, keys_z + 1, all_z)
    behind = hartley(keys_z, keys_z - 1, all_z)
    into_z = jnp.asarray(table_z.reshape(all_z, size_g, nz).transpose(1, 0, 2), jnp.float32)
    pull_z = -0.5 * (ahead - behind)
    from_z = np.concatenate(
        [t.reshape(all_z, size_g, nz).transpose(1, 0, 2) for t in (table_z, pull_z)], axis=2
    )
    from_z = jnp.asarray(from_z, jnp.float32)
    keys_y = np.arange(all_y)
    table_y = jnp.asarray(hartley(keys_y, keys_y, all_y), jnp.float32)
    tables = jnp.asarray(decay_tables(all_x, all_y, all_z))
    flat_table = jnp.asarray(flat_mode_table(nx, all_x, all_y, all_z))

    floats = functools.partial(pltpu.VMEM, dtype=jnp.float32)

    spectral, den, vel, pre, spe, cnt = placed_call(
        first_kernel,
        (density, velocity, pressure, species, newton_count, into_z),
        "hhhhhh",
        [(all_z, main), density.shape, velocity.shape, pressure.shape, species.shape, newton_count],
        OUT_FIRST,
        [floats((all_z, nz)), pltpu.SemaphoreType.DMA((2, 4))],
    )
    spectral = lax.all_to_all(spectral.reshape(groups, kz, main), ("hy", "ga"), split_axis=0, concat_axis=0, tiled=True)
    cooled, dense, sound, xfirst, xlast, ylo, yhi, zface, own_y, own_decay, own_flat = placed_call(
        pack_kernel,
        (den, vel, pre, spe, cnt, table_y, tables, flat_table),
        "vvvvvhhh",
        [pre.shape, spe.shape, pre.shape] + [(prim_n, ny, nz)] * 2 + [(prim_n, nx, nz)] * 2 + [(nx, ny, LANES)]
        + [table_y.shape, (3, kz, all_y), flat_table.shape],
        OUT_PACK,
        [pltpu.SemaphoreType.DMA((3,))],
        {2: 0, 3: 1},
    )
    modes, sums = placed_call(
        functools.partial(along_y_kernel, size_g, ny),
        (spectral, own_y, own_decay),
        IN_Y,
        [(nx, kz, all_y), (2 * kz + nx, all_y)],
        OUT_Y,
        [floats((nx * kz, all_y))],
    )
    others = []
    for step in range(1, size_x):
        others.append(exchanged(sums, "hx", step))
    ybelow = shifted(yhi, "hy", 1)
    yabove = shifted(ylo, "hy", -1)
    zbelow = shifted(zface, "ga", 1)
    zabove = zbelow if size_g == 2 else shifted(zface, "ga", -1)
    xfirst = faced_pairs(xfirst, "hx", True)
    xlast = faced_pairs(xlast, "hx", False)
    (planes,) = placed_call(
        functools.partial(along_x_kernel, size_x, size_g, ny),
        (modes, sums, *others, own_y, own_decay, own_flat),
        "v-" + IN_OTHERS * (size_x - 1) + "vvv",
        [(groups, kz, width)],
        OUT_X,
        [
            floats((size_x, 2 * kz + nx, all_y)),
            floats((all_x, all_y)),
            floats(((nx + 2) * kz, all_y)),
            floats(((nx + 2) * kz, all_y)),
        ],
    )
    planes = lax.all_to_all(planes, ("hy", "ga"), split_axis=0, concat_axis=0, tiled=True)
    state = (den, vel, cooled, dense, sound)
    new_density, species_mass, carried, rim, own_z = placed_call(
        flux_kernel,
        (*state, ybelow, yabove, zbelow, zabove, from_z),
        IN_FLUX,
        [
            (nx, ny, nz), (species_n, nx, ny, nz), (4, nx, ny, nz),
            (prim_n, 2, ny, nz), from_z.shape[1:],
        ],
        OUT_FLUX,
        [
            floats((1 + species_n, nx - 2, ny, nz)),
            floats((2, flow_n, nx, nz)),
            pltpu.SemaphoreType.DMA((2, nx - 2)),
            pltpu.SemaphoreType.DMA((1,)),
        ],
    )
    new_density, species_mass, carried_rim = placed_call(
        rim_kernel,
        (*state, rim, xfirst, xlast, new_density, species_mass),
        IN_RIM,
        [(nx, ny, nz), (species_n, nx, ny, nz), (4, 2, ny, nz)],
        OUT_RIM,
        [
            floats((2, prim_n, ny, nz)),
            floats((1 + species_n, 2, ny, nz)),
            pltpu.SemaphoreType.DMA((2,)),
            pltpu.SemaphoreType.DMA((2, 2)),
        ],
        {8: 0, 9: 1},
    )
    potential, momentum, total_energy = placed_call(
        gravity_kernel,
        (planes, own_z, den, vel, carried, carried_rim),
        IN_GRAVITY,
        [(nx, ny, nz), (3, nx, ny, nz), (nx, ny, nz)],
        "---",
        [floats((main, 2 * nz)), floats((LANES, nz))],
    )
    return (new_density, momentum, total_energy, species_mass, potential)


def solution(mesh):
    cells = P("hx", "hy", "ga")
    fields = P(None, "hx", "hy", "ga")
    return jax.shard_map(
        step,
        mesh=mesh,
        in_specs=(cells, fields, cells, fields, cells),
        out_specs=(cells, fields, cells, fields, cells),
        check_vma=False,
    )
```

```python
import functools
import math

import jax
import jax.numpy as jnp
import numpy as np
from jax import lax
from jax.experimental import pallas as pl
from jax.experimental.pallas import tpu as pltpu
from jax.sharding import PartitionSpec as P


NEWTON = 4
gamma_gas = 5.0 / 3.0
time_step = 0.1
cool_rates = (2.0, 5.0, 9.0, 14.0, 20.0, 3.0, 7.0, 11.0, 29.0)
species_n = len(cool_rates)
prim_n = 5 + species_n
half_step = 0.5 * time_step
highest = lax.Precision.HIGHEST
LANES = 128
GRANT = 16 * 2**20
GROUP = 2
OUT_PACK = "vvvvvvhhhhhvvv"
OUT_Y = "v-"
IN_OTHERS = "-"
OUT_X = "h"
IN_FLUX = "vvvvvvvvvh"
OUT_FLUX = "xxvvv"
IN_RIM = "vvvvvvhhhh"
OUT_RIM = "xxv"
IN_GRAVITY = "-vvvvv"
P_AT = 4
C_AT = prim_n
face_n = prim_n + 3


def sound_speed(density, pressure):
    return jnp.sqrt(gamma_gas * pressure / density)


def conserved(kept):
    density, v0, v1, v2, pressure = kept[:5]
    energy = pressure * (1.0 / (gamma_gas - 1.0)) + 0.5 * density * (v0 * v0 + v1 * v1 + v2 * v2)
    return [density, density * v0, density * v1, density * v2, energy] + list(kept[5:prim_n])


def cooled_plane(density, pressure, species, count):
    cooling = cool_rates[0] * species[0]
    for s in range(1, species_n):
        cooling = cooling + cool_rates[s] * species[s]
    stiffness = time_step * density * cooling
    initial = pressure / ((gamma_gas - 1.0) * density)
    energy = initial
    for step in range(NEWTON):
        above = 1.0 + energy
        residual = ((energy - initial) * above + stiffness * energy * energy) * above
        derivative = above * above + stiffness * energy * (energy + 2.0)
        energy = jnp.where(count > step, energy - residual / derivative, energy)
    return (gamma_gas - 1.0) * density * energy


def copies_in(pairs, semaphores):
    started = []
    for n, (source, target) in enumerate(pairs):
        copy = pltpu.make_async_copy(source, target, semaphores.at[n])
        copy.start()
        started.append(copy)
    return started


def primitive_plane(x, den, vel, pre, spe, cnt):
    density = den[x]
    species = [spe[s, x] for s in range(species_n)]
    pressure = cooled_plane(density, pre[x], species, cnt[x])
    return [density, vel[0, x], vel[1, x], vel[2, x], pressure] + [density * s for s in species]


def place_in_plane():
    in_g = lax.axis_index("ga")
    return in_g, in_g * lax.axis_size("hy") + lax.axis_index("hy")


def along_z_kernel(count_g, count_y, den, *rest):
    others, (table, *outs, spectrum) = rest[: count_g - 1], rest[count_g - 1 :]
    nx, ny, nz = den.shape
    me = lax.axis_index("ga")
    total = None
    for step in range(count_g):
        cells = den if step == 0 else others[step - 1]
        part = lax.dot_general(
            table[source_of(me, step, count_g)], cells[...].reshape(nx * ny, nz),
            (((1,), (1,)), ((), ())), precision=highest, preferred_element_type=jnp.float32,
        )
        total = part if step == 0 else total + part
    spectrum[...] = total
    kz = outs[0].shape[0]
    row = lax.axis_index("hy")
    for step, out in enumerate(outs):
        out[...] = spectrum[pl.ds(target_of(row, step, count_y) * kz, kz), :]


def pack_kernel(den_at, vel_at, pre_at, spe_at, cnt_at, into_z, table_y, tables, flat_table, into,
                den, vel, cooled, mass, sound, xfirst, xlast, ylo, yhi, zface, own_y, own_decay, own_flat,
                cnt, gas_semaphores, semaphores):
    nx, ny, nz = den.shape
    kz = own_decay.shape[1]
    in_g, place = place_in_plane()
    parts = []
    for n in range(2):
        half = pl.ds(n * (nx // 2), nx // 2)
        parts.append(
            copies_in(
                [
                    (den_at.at[half], den.at[half]),
                    (pre_at.at[half], cooled.at[half]),
                    (cnt_at.at[half], cnt.at[half]),
                    (spe_at.at[:, half], mass.at[:, half]),
                    (vel_at.at[:, half], vel.at[:, half]),
                ],
                gas_semaphores.at[n],
            )
        )
    lane = lax.broadcasted_iota(jnp.int32, (ny, LANES), 1)
    later = copies_in(
        [
            (into_z.at[in_g], into),
            (table_y, own_y),
            (tables.at[:, pl.ds(place * kz, kz), :], own_decay),
            (flat_table, own_flat),
        ],
        semaphores,
    )

    second, _ = face_roles("hx")

    def plane(x):
        primitive = primitive_plane(x, den, vel, cooled, mass, cnt)
        kept = primitive + [sound_speed(primitive[0], primitive[P_AT])]
        cooled[x] = kept[P_AT]
        for s in range(species_n):
            mass[s, x] = kept[P_AT + 1 + s]
        sound[x] = kept[C_AT]
        carried = conserved(kept) + [kept[P_AT], kept[C_AT], kept[3]]
        packed = jnp.zeros((ny, LANES), jnp.float32)
        for c in range(face_n):
            packed = jnp.where(lane // 2 == c, pltpu.roll(carried[c], 2 * c + 1, 1), packed)
        zface[x] = packed

    def planes(i, _):
        for n in range(GROUP):
            plane(i * GROUP + n)
        return 0

    turns = nx // 2 // GROUP
    for n, copies in enumerate(parts):
        for copy in copies:
            copy.wait()
        lax.fori_loop(n * turns, (n + 1) * turns, planes, 0)
    kept = [den] + [vel.at[d] for d in range(3)] + [cooled] + [mass.at[s] for s in range(species_n)]
    for c in range(prim_n):
        rows = kept[c].reshape(nx * ny, nz)
        ylo[c] = rows[pl.ds(0, nx, stride=ny), :]
        yhi[c] = rows[pl.ds(ny - 1, nx, stride=ny), :]
        xfirst[c] = kept[c][(nx - 1) * (1 - second)]
        xlast[c] = kept[c][(nx - 1) * second]
    for copy in later:
        copy.wait()


flow_p, flow_c, flow_v = prim_n, prim_n + 1, prim_n + 2
flow_n = prim_n + 5


def with_flow(kept):
    return conserved(kept) + [kept[P_AT], kept[C_AT], kept[1], kept[2], kept[3]]


def faced(face):
    kept = [face[c] for c in range(prim_n)]
    return with_flow(kept + [sound_speed(kept[0], kept[P_AT])])


def stored(x, den, vel, cooled, dense, speed_of):
    kept = [den[x], vel[0, x], vel[1, x], vel[2, x], cooled[x]]
    return with_flow(kept + [dense[s, x] for s in range(species_n)] + [speed_of[x]])


def flux_kernel(den, vel, cooled, dense, speed_of, ybelow, yabove, zbelow, zabove, from_z,
                new_density, mass, carried, rim, own_z, ready, yedge, out_semaphores, semaphores):
    nx, ny, nz = den.shape
    row = lax.broadcasted_iota(jnp.int32, (ny, nz), 0)
    lane = lax.broadcasted_iota(jnp.int32, (ny, nz), 1)
    copies = copies_in([(from_z.at[place_in_plane()[0]], own_z)], semaphores)
    state = (den, vel, cooled, dense, speed_of)
    for side, face in enumerate((ybelow, yabove)):
        for f, value in enumerate(faced(face)):
            yedge[side, f] = value

    def plane(x, lower, upper):
        from_below = zbelow[x]
        from_above = zabove[x]
        centre = stored(x, *state)

        def beside(f, direction, up):
            if direction == 0:
                return upper[f] if up else lower[f]
            here = centre[f]
            if direction == 1:
                edge = yedge[1 if up else 0, f, pl.ds(x, 1), :]
                if up:
                    return jnp.where(row == ny - 1, edge, pltpu.roll(here, ny - 1, 0))
                return jnp.where(row == 0, edge, pltpu.roll(here, 1, 0))
            slot = f if f < flow_v else flow_v
            if up:
                edge = pltpu.roll(from_above, (LANES - 2 - 2 * slot) % LANES, 1)
                return jnp.where(lane == nz - 1, edge, pltpu.roll(here, nz - 1, 1))
            edge = pltpu.roll(from_below, (LANES - 2 * slot) % LANES, 1)
            return jnp.where(lane == 0, edge, pltpu.roll(here, 1, 1))

        stay, work = 1.0, 0.0
        weights, push = [], []
        for d in range(3):
            speed = jnp.abs(centre[flow_v + d]) + centre[flow_c]
            pushed = 0.0
            for up in (False, True):
                if d == 0 and (upper if up else lower) is None:
                    continue
                sign = -1.0 if up else 1.0
                v, p = beside(flow_v + d, d, up), beside(flow_p, d, up)
                signal = jnp.maximum(speed, jnp.abs(v) + beside(flow_c, d, up))
                stay = stay - half_step * signal
                weights.append((d, up, half_step * (signal + sign * v)))
                pushed = pushed + sign * half_step * p
                work = work + sign * half_step * (p * v)
            push.append(pushed)

        def updated(f):
            total = stay * centre[f]
            for d, up, weight in weights:
                total = total + weight * beside(f, d, up)
            return total

        result = [updated(f) for f in range(prim_n)]
        for d in range(3):
            result[1 + d] = result[1 + d] + push[d]
        result[4] = result[4] + work
        return result

    def leave(x):
        return [
            pltpu.make_async_copy(ready.at[0, x - 1], new_density.at[x], out_semaphores.at[0, x - 1]),
            pltpu.make_async_copy(
                ready.at[pl.ds(1, species_n), x - 1], mass.at[:, x], out_semaphores.at[1, x - 1]
            ),
        ]

    def inner(x, _):
        result = plane(x, stored(x - 1, *state), stored(x + 1, *state))
        ready[0, x - 1] = result[0]
        for d in range(4):
            carried[d, x] = result[1 + d]
        for s in range(species_n):
            ready[1 + s, x - 1] = result[5 + s]
        for copy in leave(x):
            copy.start()
        return 0

    def left(x, _):
        for copy in leave(x):
            copy.wait()
        return 0

    lax.fori_loop(1, nx - 1, inner, 0)
    for f, value in enumerate(plane(0, None, stored(1, *state))):
        rim[f, 0] = value
    for f, value in enumerate(plane(nx - 1, stored(nx - 2, *state), None)):
        rim[f, 1] = value
    for copy in copies:
        copy.wait()
    lax.fori_loop(1, nx - 1, left, 0)


def rim_kernel(den, vel, cooled, dense, speed_of, rim, xfirst, xlast, density_in, mass_in,
               new_density, mass, carried_rim, xfaces, ready, semaphores, out_semaphores):
    nx, _, _ = den.shape
    _, slot = face_roles("hx")
    copies = copies_in([(xfirst, xfaces.at[slot]), (xlast, xfaces.at[1 - slot])], semaphores)
    for copy in copies:
        copy.wait()
    leaving = []
    for n, (x, sign) in enumerate(((0, 1.0), (nx - 1, -1.0))):
        centre = stored(x, den, vel, cooled, dense, speed_of)
        other = faced(xfaces.at[n])
        v, p = other[flow_v], other[flow_p]
        signal = jnp.maximum(jnp.abs(centre[flow_v]) + centre[flow_c], jnp.abs(v) + other[flow_c])
        lost, weight = half_step * signal, half_step * (signal + sign * v)
        result = [rim[f, n] - lost * centre[f] + weight * other[f] for f in range(prim_n)]
        result[1] = result[1] + sign * half_step * p
        result[4] = result[4] + sign * half_step * (p * v)
        ready[0, n] = result[0]
        for d in range(4):
            carried_rim[d, n] = result[1 + d]
        for s in range(species_n):
            ready[1 + s, n] = result[5 + s]
        leaving += copies_in(
            [(ready.at[0, n], new_density.at[x]), (ready.at[pl.ds(1, species_n), n], mass.at[:, x])],
            out_semaphores.at[n],
        )
    for copy in leaving:
        copy.wait()


SPACES = {"h": pltpu.HBM, "v": pltpu.VMEM, "x": pltpu.HBM}


def placed_call(kernel, inputs, in_spaces, outputs, out_spaces, scratch, aliases={}):
    specs, operands = [], []
    for value, space in zip(inputs, in_spaces, strict=True):
        specs.append(pl.BlockSpec(memory_space=pl.ANY if space == "h" else pltpu.VMEM))
        if space != "-":
            value = pltpu.with_memory_space_constraint(value, SPACES[space])
        operands.append(value)
    shapes = []
    for shape, space in zip(outputs, out_spaces, strict=True):
        shape, kind = (shape, jnp.float32) if isinstance(shape, tuple) else (shape.shape, shape.dtype)
        shapes.append(jax.ShapeDtypeStruct(shape, kind) if space == "-" else SPACES[space](shape, kind))
    return pl.pallas_call(
        kernel,
        out_shape=shapes,
        in_specs=specs,
        out_specs=[pl.BlockSpec(memory_space=pl.ANY if space == "x" else pltpu.VMEM) for space in out_spaces],
        scratch_shapes=scratch,
        input_output_aliases=aliases,
        compiler_params=pltpu.CompilerParams(vmem_limit_bytes=GRANT),
    )(*operands)


def exchanged(value, axis, step):
    count = lax.axis_size(axis)
    return lax.ppermute(value, axis, [(i, partner(i, step, count)) for i in range(count)])


def partner(index, step, count):
    return index ^ step if count & (count - 1) == 0 else (index + step) % count


def target_of(index, step, count):
    return index ^ step if count & (count - 1) == 0 else lax.rem(index + step, count)


def source_of(index, step, count):
    return index ^ step if count & (count - 1) == 0 else lax.rem(index + count - step, count)


def face_roles(axis):
    if lax.axis_size(axis) % 2:
        return 0, 0
    second = lax.rem(lax.axis_index(axis), 2)
    return second, 1 - second


def faced_pairs(value, axis, first_round):
    count = lax.axis_size(axis)
    if count % 2:
        return shifted(value, axis, 1 if first_round else -1)
    start = 0 if first_round else 1
    pairs = [((start + i) % count, (start + i + 1) % count) for i in range(0, count, 2)]
    return lax.ppermute(value, axis, pairs + [(b, a) for a, b in pairs])


def shifted(value, axis, step):
    count = lax.axis_size(axis)
    return lax.ppermute(value, axis, [(i, (i + step) % count) for i in range(count)])


def hartley(rows, columns, length):
    angle = 2.0 * np.pi / length * (np.outer(rows, columns) % length)
    return np.cos(angle) + np.sin(angle)


def curvature(length):
    return 4.0 * np.sin(np.pi / length * np.arange(length)) ** 2


def decay_tables(nx, ny, nz):
    mu = curvature(nz)[:, None] + curvature(ny)[None, :]
    mu[0, 0] = 1.0
    root = np.sqrt(mu * (4.0 + mu))
    decay = 2.0 / (2.0 + mu + root)
    return np.stack([decay, 1.0 / (1.0 - decay**nx), -1.0 / (root * ny * nz)]).astype(np.float32)


def flat_mode_table(block, nx, ny, nz):
    rows = -(-(block + 2) // 8) * 8
    cell = np.arange(-1, rows - 1)[:, None]
    segment = np.arange(nx // block)[:, None]
    source = (np.arange(block)[None, :] - block * segment).reshape(1, -1)
    gap = (cell - source) % nx
    table = gap * (nx - gap) / (2.0 * nx) - (nx * nx - 1.0) / (12.0 * nx)
    return (table / (ny * nz)).astype(np.float32)


def segments(kz, width):
    return lax.broadcasted_iota(jnp.int32, (kz, LANES), 1) // width


def turned(value, lanes):
    lanes = lanes % LANES
    return pltpu.roll(value, lanes, 1) if lanes else value


def along_y_kernel(count, block, *rest):
    received, (table_y, tables, modes, sums, grid_rows, lines) = rest[:count], rest[count:]
    for step in range(count):
        lines[source_of(lax.axis_index("hy"), step, count)] = received[step][...]
    kz = lines.shape[1]
    nx, _, ny = modes.shape
    width = block
    per = LANES // width
    place = segments(kz, width)
    for column in range(ny // LANES):
        for high in range(nx // per):
            source = []
            for s in range(per):
                source.append(lines[column * per + s, :, high * LANES : (high + 1) * LANES])
            for low in range(per):
                line = turned(source[0], -low * width)
                for s in range(1, per):
                    line = jnp.where(place == s, turned(source[s], (s - low) * width), line)
                x = high * per + low
                grid_rows[x * kz : (x + 1) * kz, column * LANES : (column + 1) * LANES] = line
    spectrum = jnp.dot(
        grid_rows[...], table_y[...], precision=highest, preferred_element_type=jnp.float32
    )
    modes[...] = spectrum.reshape(nx, kz, ny)
    decay = tables[0]
    forward, backward = modes[0], modes[nx - 1]
    for x in range(1, nx):
        forward = forward * decay + modes[x]
        backward = backward * decay + modes[nx - 1 - x]
    sums[0:kz] = forward
    sums[kz : 2 * kz] = backward
    for x in range(nx):
        sums[2 * kz + x : 2 * kz + x + 1] = modes[x, 0:1, :]


def along_x_kernel(count, size_g, block, modes, own, *rest):
    others = rest[: count - 1]
    table_y, tables, flat_table, out, everyone, gathered, potential, lines = rest[count - 1 :]
    me = lax.axis_index("hx")
    everyone[me] = own[...]
    for step in range(1, count):
        everyone[source_of(me, step, count)] = others[step - 1][...]

    def seen(distance):
        return everyone.at[lax.rem(me + count - distance, count)]

    nx, kz, ny = modes.shape
    width = block
    per = LANES // width
    for s in range(count):
        gathered[s * nx : (s + 1) * nx] = seen(s)[2 * kz : 2 * kz + nx]
    flat = jnp.dot(
        flat_table[...], gathered[...], precision=highest, preferred_element_type=jnp.float32
    )
    for tile in range(0, kz, 8):
        rows = slice(tile, tile + 8)
        decay, closing, scale = tables[0, rows], tables[1, rows], tables[2, rows]
        far = decay
        for _ in range(int(math.log2(nx))):
            far = far * far
        left = own[tile : tile + 8]
        right = own[kz + tile : kz + tile + 8]
        for s in range(count - 1, 0, -1):
            left = left * far + seen(s)[tile : tile + 8]
            right = right * far + seen(count - s)[kz + tile : kz + tile + 8]
        left, right = left * closing, right * closing
        from_left = [left]
        for x in range(nx):
            from_left.append(from_left[-1] * decay + modes[x, rows])
        result = [None] * (nx + 2)
        result[nx + 1] = from_left[nx] * decay + right
        behind = right
        for x in range(nx - 1, -1, -1):
            result[x + 1] = behind * decay + from_left[x + 1]
            behind = behind * decay + modes[x, rows]
        result[0] = from_left[0] + behind * decay
        if tile == 0:
            first = lax.broadcasted_iota(jnp.int32, (8, ny), 0) + lax.broadcasted_iota(jnp.int32, (8, ny), 1)
            first = first + place_in_plane()[1] == 0
        for x in range(nx + 2):
            value = result[x] * scale
            if tile == 0:
                value = jnp.where(first, flat[x : x + 1, :], value)
            potential[x * kz + tile : x * kz + tile + 8] = value
    lines[...] = jnp.dot(
        potential[...], table_y[...], precision=highest, preferred_element_type=jnp.float32
    )
    place = segments(kz, width)
    lane = lax.broadcasted_iota(jnp.int32, (kz, LANES), 1)

    def line(x, column):
        return lines[(x + 1) * kz : (x + 2) * kz, column * LANES : (column + 1) * LANES]

    for target in range(ny // width):
        column, s = target // per, target % per
        pieces = []
        for high in range(nx // per):
            piece = turned(line(high * per, column), -s * width)
            for low in range(1, per):
                piece = jnp.where(place == low, turned(line(high * per + low, column), (low - s) * width), piece)
            pieces.append(piece)
        edge = turned(line(-1, column), -s * width)
        edge = jnp.where(place == 1, turned(line(nx, column), (1 - s) * width), edge)
        for side, y in enumerate((target * width - 1, (target + 1) * width)):
            y = y % ny
            for x in range(nx):
                slot = 2 * width + side * nx + x
                edge = jnp.where(lane == slot, turned(line(x, y // LANES), slot - y % LANES), edge)
        pieces.append(edge)
        for g in range(size_g):
            for p, piece in enumerate(pieces):
                out[target * size_g + g, :, p * LANES : (p + 1) * LANES] = piece


def gravity_kernel(planes, table, den, vel, carried, carried_rim, potential, momentum, energy, solved, edges):
    nx, ny, nz = den.shape
    groups, kz, width = planes.shape
    main = nx * ny
    flat = planes[...].reshape(groups * kz, width)
    here = table[...]
    contract = (((0,), (0,)), ((), ()))
    solved[...] = lax.dot_general(
        flat[:, :main], here, contract, precision=highest, preferred_element_type=jnp.float32
    )
    edges[...] = lax.dot_general(
        flat[:, main:], here[:, :nz], contract, precision=highest, preferred_element_type=jnp.float32
    )
    row = lax.broadcasted_iota(jnp.int32, (ny, nz), 0)
    for x in range(nx):
        value = solved[x * ny : (x + 1) * ny, :nz]
        potential[x] = value
        above = solved[(x + 1) * ny : (x + 2) * ny, :nz] if x < nx - 1 else edges[ny : 2 * ny]
        below = solved[(x - 1) * ny : x * ny, :nz] if x > 0 else edges[:ny]
        at = 2 * ny + x
        right = jnp.where(row == ny - 1, edges[at + nx : at + nx + 1], pltpu.roll(value, ny - 1, 0))
        left = jnp.where(row == 0, edges[at : at + 1], pltpu.roll(value, 1, 0))
        pull = time_step * den[x]
        kicks = [
            pull * (-0.5 * (above - below)),
            pull * (-0.5 * (right - left)),
            pull * solved[x * ny : (x + 1) * ny, nz:],
        ]
        before = [carried_rim[d, x // (nx - 1)] if x in (0, nx - 1) else carried[d, x] for d in range(4)]
        work = before[3]
        for d in range(3):
            momentum[d, x] = before[d] + kicks[d]
            work = work + kicks[d] * vel[d, x]
        energy[x] = work


def step(density, velocity, pressure, species, newton_count):
    size_x, size_y, size_g = (lax.axis_size(a) for a in ("hx", "hy", "ga"))
    nx, ny, nz = density.shape
    all_x, all_y, all_z = nx * size_x, ny * size_y, nz * size_g
    groups = size_y * size_g
    kz = all_z // groups
    main = nx * ny
    width = main + LANES

    keys_z = np.arange(all_z)
    table_z = hartley(keys_z, keys_z, all_z)
    ahead = hartley(keys_z, keys_z + 1, all_z)
    behind = hartley(keys_z, keys_z - 1, all_z)
    into_z = table_z.reshape(size_g, all_z // size_g, size_g, nz).transpose(0, 2, 1, 3)
    into_z = jnp.asarray(into_z, jnp.float32)
    pull_z = -0.5 * (ahead - behind)
    from_z = np.concatenate(
        [t.reshape(all_z, size_g, nz).transpose(1, 0, 2) for t in (table_z, pull_z)], axis=2
    )
    from_z = from_z.reshape(size_g, size_g, size_y, kz, 2 * nz).transpose(0, 2, 1, 3, 4)
    from_z = jnp.asarray(from_z.reshape(size_g, all_z, 2 * nz), jnp.float32)
    keys_y = np.arange(all_y)
    table_y = jnp.asarray(hartley(keys_y, keys_y, all_y), jnp.float32)
    tables = jnp.asarray(decay_tables(all_x, all_y, all_z))
    flat_table = jnp.asarray(flat_mode_table(nx, all_x, all_y, all_z))

    floats = functools.partial(pltpu.VMEM, dtype=jnp.float32)

    near_density = [exchanged(density, "ga", step) for step in range(1, size_g)]
    into, den, vel, cooled, dense, sound, xfirst, xlast, ylo, yhi, zface, own_y, own_decay, own_flat = placed_call(
        pack_kernel,
        (density, velocity, pressure, species, newton_count, into_z, table_y, tables, flat_table),
        "hhhhhhhhh",
        [into_z.shape[1:], density.shape, velocity.shape, pressure.shape, species.shape, density.shape]
        + [(prim_n, ny, nz)] * 2 + [(prim_n, nx, nz)] * 2 + [(nx, ny, LANES)]
        + [table_y.shape, (3, kz, all_y), flat_table.shape],
        OUT_PACK,
        [
            pltpu.VMEM((nx, ny, nz), jnp.int32),
            pltpu.SemaphoreType.DMA((2, 5)),
            pltpu.SemaphoreType.DMA((4,)),
        ],
    )
    spectral = placed_call(
        functools.partial(along_z_kernel, size_g, size_y),
        (den, *near_density, into),
        "v" + "-" * (size_g - 1) + "v",
        [(kz, main)] * size_y,
        "-" * size_y,
        [floats((all_z // size_g, main))],
    )
    spectral = list(spectral)
    for step in range(1, size_y):
        spectral[step] = exchanged(spectral[step], "hy", step)
    modes, sums = placed_call(
        functools.partial(along_y_kernel, size_y, ny),
        (*spectral, own_y, own_decay),
        "-" * size_y + "vv",
        [(nx, kz, all_y), (2 * kz + nx, all_y)],
        OUT_Y,
        [floats((nx * kz, all_y)), floats((size_y, kz, main))],
    )
    ybelow = shifted(yhi, "hy", 1)
    yabove = shifted(ylo, "hy", -1)
    zbelow = shifted(zface, "ga", 1)
    zabove = zbelow if size_g == 2 else shifted(zface, "ga", -1)
    others = []
    for step in range(1, size_x):
        others.append(exchanged(sums, "hx", step))
    xfirst = faced_pairs(xfirst, "hx", True)
    xlast = faced_pairs(xlast, "hx", False)
    (planes,) = placed_call(
        functools.partial(along_x_kernel, size_x, size_g, ny),
        (modes, sums, *others, own_y, own_decay, own_flat),
        "v-" + IN_OTHERS * (size_x - 1) + "vvv",
        [(groups, kz, width)],
        OUT_X,
        [
            floats((size_x, 2 * kz + nx, all_y)),
            floats((all_x, all_y)),
            floats(((nx + 2) * kz, all_y)),
            floats(((nx + 2) * kz, all_y)),
        ],
    )
    planes = lax.all_to_all(planes, ("hy", "ga"), split_axis=0, concat_axis=0, tiled=True)
    state = (den, vel, cooled, dense, sound)
    new_density, species_mass, carried, rim, own_z = placed_call(
        flux_kernel,
        (*state, ybelow, yabove, zbelow, zabove, from_z),
        IN_FLUX,
        [
            (nx, ny, nz), (species_n, nx, ny, nz), (4, nx, ny, nz),
            (prim_n, 2, ny, nz), from_z.shape[1:],
        ],
        OUT_FLUX,
        [
            floats((1 + species_n, nx - 2, ny, nz)),
            floats((2, flow_n, nx, nz)),
            pltpu.SemaphoreType.DMA((2, nx - 2)),
            pltpu.SemaphoreType.DMA((1,)),
        ],
    )
    new_density, species_mass, carried_rim = placed_call(
        rim_kernel,
        (*state, rim, xfirst, xlast, new_density, species_mass),
        IN_RIM,
        [(nx, ny, nz), (species_n, nx, ny, nz), (4, 2, ny, nz)],
        OUT_RIM,
        [
            floats((2, prim_n, ny, nz)),
            floats((1 + species_n, 2, ny, nz)),
            pltpu.SemaphoreType.DMA((2,)),
            pltpu.SemaphoreType.DMA((2, 2)),
        ],
        {8: 0, 9: 1},
    )
    potential, momentum, total_energy = placed_call(
        gravity_kernel,
        (planes, own_z, den, vel, carried, carried_rim),
        IN_GRAVITY,
        [(nx, ny, nz), (3, nx, ny, nz), (nx, ny, nz)],
        "---",
        [floats((main, 2 * nz)), floats((LANES, nz))],
    )
    return (new_density, momentum, total_energy, species_mass, potential)


def solution(mesh):
    cells = P("hx", "hy", "ga")
    fields = P(None, "hx", "hy", "ga")
    return jax.shard_map(
        step,
        mesh=mesh,
        in_specs=(cells, fields, cells, fields, cells),
        out_specs=(cells, fields, cells, fields, cells),
        check_vma=False,
    )
```

```python
import functools
import math

import jax
import jax.numpy as jnp
import numpy as np
from jax import lax
from jax.experimental import pallas as pl
from jax.experimental.pallas import tpu as pltpu
from jax.sharding import PartitionSpec as P


NEWTON = 4
gamma_gas = 5.0 / 3.0
time_step = 0.1
cool_rates = (2.0, 5.0, 9.0, 14.0, 20.0, 3.0, 7.0, 11.0, 29.0)
species_n = len(cool_rates)
prim_n = 5 + species_n
half_step = 0.5 * time_step
highest = lax.Precision.HIGHEST
LANES = 128
GRANT = 16 * 2**20
GROUP = 2
OUT_PACK = "vvvvvvhhhhhvvv"
OUT_Y = "v-"
IN_OTHERS = "-"
OUT_X = "x"
IN_FLUX = "vvvvvvvvvh"
OUT_FLUX = "xxvvv"
IN_RIM = "vvvvvvhhhh"
OUT_RIM = "xxv"
IN_GRAVITY = "-vvvvv"
P_AT = 4
C_AT = prim_n
face_n = prim_n + 3


def sound_speed(density, pressure):
    return jnp.sqrt(gamma_gas * pressure / density)


def conserved(kept):
    density, v0, v1, v2, pressure = kept[:5]
    energy = pressure * (1.0 / (gamma_gas - 1.0)) + 0.5 * density * (v0 * v0 + v1 * v1 + v2 * v2)
    return [density, density * v0, density * v1, density * v2, energy] + list(kept[5:prim_n])


def cooled_plane(density, pressure, species, count):
    cooling = cool_rates[0] * species[0]
    for s in range(1, species_n):
        cooling = cooling + cool_rates[s] * species[s]
    stiffness = time_step * density * cooling
    initial = pressure / ((gamma_gas - 1.0) * density)
    energy = initial
    for step in range(NEWTON):
        above = 1.0 + energy
        residual = ((energy - initial) * above + stiffness * energy * energy) * above
        derivative = above * above + stiffness * energy * (energy + 2.0)
        energy = jnp.where(count > step, energy - residual / derivative, energy)
    return (gamma_gas - 1.0) * density * energy


def copies_in(pairs, semaphores):
    started = []
    for n, (source, target) in enumerate(pairs):
        copy = pltpu.make_async_copy(source, target, semaphores.at[n])
        copy.start()
        started.append(copy)
    return started


def primitive_plane(x, den, vel, pre, spe, cnt):
    density = den[x]
    species = [spe[s, x] for s in range(species_n)]
    pressure = cooled_plane(density, pre[x], species, cnt[x])
    return [density, vel[0, x], vel[1, x], vel[2, x], pressure] + [density * s for s in species]


def place_in_plane():
    in_g = lax.axis_index("ga")
    return in_g, in_g * lax.axis_size("hy") + lax.axis_index("hy")


def along_z_kernel(count_g, count_y, den, *rest):
    others, (table, *outs, spectrum) = rest[: count_g - 1], rest[count_g - 1 :]
    nx, ny, nz = den.shape
    me = lax.axis_index("ga")
    total = None
    for step in range(count_g):
        cells = den if step == 0 else others[step - 1]
        part = lax.dot_general(
            table[source_of(me, step, count_g)], cells[...].reshape(nx * ny, nz),
            (((1,), (1,)), ((), ())), precision=highest, preferred_element_type=jnp.float32,
        )
        total = part if step == 0 else total + part
    spectrum[...] = total
    kz = outs[0].shape[0]
    row = lax.axis_index("hy")
    for step, out in enumerate(outs):
        out[...] = spectrum[pl.ds(target_of(row, step, count_y) * kz, kz), :]


def pack_kernel(den_at, vel_at, pre_at, spe_at, cnt_at, into_z, table_y, tables, flat_table, into,
                den, vel, cooled, mass, sound, xfirst, xlast, ylo, yhi, zface, own_y, own_decay, own_flat,
                cnt, gas_semaphores, semaphores):
    nx, ny, nz = den.shape
    kz = own_decay.shape[1]
    in_g, place = place_in_plane()
    parts = []
    for n in range(2):
        half = pl.ds(n * (nx // 2), nx // 2)
        parts.append(
            copies_in(
                [
                    (den_at.at[half], den.at[half]),
                    (pre_at.at[half], cooled.at[half]),
                    (cnt_at.at[half], cnt.at[half]),
                    (spe_at.at[:, half], mass.at[:, half]),
                    (vel_at.at[:, half], vel.at[:, half]),
                ],
                gas_semaphores.at[n],
            )
        )
    lane = lax.broadcasted_iota(jnp.int32, (ny, LANES), 1)
    later = copies_in(
        [
            (into_z.at[in_g], into),
            (table_y, own_y),
            (tables.at[:, pl.ds(place * kz, kz), :], own_decay),
            (flat_table, own_flat),
        ],
        semaphores,
    )

    second, _ = face_roles("hx")

    def plane(x):
        primitive = primitive_plane(x, den, vel, cooled, mass, cnt)
        kept = primitive + [sound_speed(primitive[0], primitive[P_AT])]
        cooled[x] = kept[P_AT]
        for s in range(species_n):
            mass[s, x] = kept[P_AT + 1 + s]
        sound[x] = kept[C_AT]
        carried = conserved(kept) + [kept[P_AT], kept[C_AT], kept[3]]
        packed = jnp.zeros((ny, LANES), jnp.float32)
        for c in range(face_n):
            packed = jnp.where(lane // 2 == c, pltpu.roll(carried[c], 2 * c + 1, 1), packed)
        zface[x] = packed

    def planes(i, _):
        for n in range(GROUP):
            plane(i * GROUP + n)
        return 0

    turns = nx // 2 // GROUP
    for n, copies in enumerate(parts):
        for copy in copies:
            copy.wait()
        lax.fori_loop(n * turns, (n + 1) * turns, planes, 0)
    kept = [den] + [vel.at[d] for d in range(3)] + [cooled] + [mass.at[s] for s in range(species_n)]
    for c in range(prim_n):
        rows = kept[c].reshape(nx * ny, nz)
        ylo[c] = rows[pl.ds(0, nx, stride=ny), :]
        yhi[c] = rows[pl.ds(ny - 1, nx, stride=ny), :]
        xfirst[c] = kept[c][(nx - 1) * (1 - second)]
        xlast[c] = kept[c][(nx - 1) * second]
    for copy in later:
        copy.wait()


flow_p, flow_c, flow_v = prim_n, prim_n + 1, prim_n + 2
flow_n = prim_n + 5


def with_flow(kept):
    return conserved(kept) + [kept[P_AT], kept[C_AT], kept[1], kept[2], kept[3]]


def faced(face):
    kept = [face[c] for c in range(prim_n)]
    return with_flow(kept + [sound_speed(kept[0], kept[P_AT])])


def stored(x, den, vel, cooled, dense, speed_of):
    kept = [den[x], vel[0, x], vel[1, x], vel[2, x], cooled[x]]
    return with_flow(kept + [dense[s, x] for s in range(species_n)] + [speed_of[x]])


def flux_kernel(den, vel, cooled, dense, speed_of, ybelow, yabove, zbelow, zabove, from_z,
                new_density, mass, carried, rim, own_z, ready, yedge, out_semaphores, semaphores):
    nx, ny, nz = den.shape
    row = lax.broadcasted_iota(jnp.int32, (ny, nz), 0)
    lane = lax.broadcasted_iota(jnp.int32, (ny, nz), 1)
    copies = copies_in([(from_z.at[place_in_plane()[0]], own_z)], semaphores)
    state = (den, vel, cooled, dense, speed_of)
    for side, face in enumerate((ybelow, yabove)):
        for f, value in enumerate(faced(face)):
            yedge[side, f] = value

    def plane(x, lower, upper):
        from_below = zbelow[x]
        from_above = zabove[x]
        centre = stored(x, *state)

        def beside(f, direction, up):
            if direction == 0:
                return upper[f] if up else lower[f]
            here = centre[f]
            if direction == 1:
                edge = yedge[1 if up else 0, f, pl.ds(x, 1), :]
                if up:
                    return jnp.where(row == ny - 1, edge, pltpu.roll(here, ny - 1, 0))
                return jnp.where(row == 0, edge, pltpu.roll(here, 1, 0))
            slot = f if f < flow_v else flow_v
            if up:
                edge = pltpu.roll(from_above, (LANES - 2 - 2 * slot) % LANES, 1)
                return jnp.where(lane == nz - 1, edge, pltpu.roll(here, nz - 1, 1))
            edge = pltpu.roll(from_below, (LANES - 2 * slot) % LANES, 1)
            return jnp.where(lane == 0, edge, pltpu.roll(here, 1, 1))

        stay, work = 1.0, 0.0
        weights, push = [], []
        for d in range(3):
            speed = jnp.abs(centre[flow_v + d]) + centre[flow_c]
            pushed = 0.0
            for up in (False, True):
                if d == 0 and (upper if up else lower) is None:
                    continue
                sign = -1.0 if up else 1.0
                v, p = beside(flow_v + d, d, up), beside(flow_p, d, up)
                signal = jnp.maximum(speed, jnp.abs(v) + beside(flow_c, d, up))
                stay = stay - half_step * signal
                weights.append((d, up, half_step * (signal + sign * v)))
                pushed = pushed + sign * half_step * p
                work = work + sign * half_step * (p * v)
            push.append(pushed)

        def updated(f):
            total = stay * centre[f]
            for d, up, weight in weights:
                total = total + weight * beside(f, d, up)
            return total

        result = [updated(f) for f in range(prim_n)]
        for d in range(3):
            result[1 + d] = result[1 + d] + push[d]
        result[4] = result[4] + work
        return result

    def leave(x):
        return [
            pltpu.make_async_copy(ready.at[0, x - 1], new_density.at[x], out_semaphores.at[0, x - 1]),
            pltpu.make_async_copy(
                ready.at[pl.ds(1, species_n), x - 1], mass.at[:, x], out_semaphores.at[1, x - 1]
            ),
        ]

    def inner(x, _):
        result = plane(x, stored(x - 1, *state), stored(x + 1, *state))
        ready[0, x - 1] = result[0]
        for d in range(4):
            carried[d, x] = result[1 + d]
        for s in range(species_n):
            ready[1 + s, x - 1] = result[5 + s]
        for copy in leave(x):
            copy.start()
        return 0

    def left(x, _):
        for copy in leave(x):
            copy.wait()
        return 0

    lax.fori_loop(1, nx - 1, inner, 0)
    for f, value in enumerate(plane(0, None, stored(1, *state))):
        rim[f, 0] = value
    for f, value in enumerate(plane(nx - 1, stored(nx - 2, *state), None)):
        rim[f, 1] = value
    for copy in copies:
        copy.wait()
    lax.fori_loop(1, nx - 1, left, 0)


def rim_kernel(den, vel, cooled, dense, speed_of, rim, xfirst, xlast, density_in, mass_in,
               new_density, mass, carried_rim, xfaces, ready, semaphores, out_semaphores):
    nx, _, _ = den.shape
    _, slot = face_roles("hx")
    copies = copies_in([(xfirst, xfaces.at[slot]), (xlast, xfaces.at[1 - slot])], semaphores)
    for copy in copies:
        copy.wait()
    leaving = []
    for n, (x, sign) in enumerate(((0, 1.0), (nx - 1, -1.0))):
        centre = stored(x, den, vel, cooled, dense, speed_of)
        other = faced(xfaces.at[n])
        v, p = other[flow_v], other[flow_p]
        signal = jnp.maximum(jnp.abs(centre[flow_v]) + centre[flow_c], jnp.abs(v) + other[flow_c])
        lost, weight = half_step * signal, half_step * (signal + sign * v)
        result = [rim[f, n] - lost * centre[f] + weight * other[f] for f in range(prim_n)]
        result[1] = result[1] + sign * half_step * p
        result[4] = result[4] + sign * half_step * (p * v)
        ready[0, n] = result[0]
        for d in range(4):
            carried_rim[d, n] = result[1 + d]
        for s in range(species_n):
            ready[1 + s, n] = result[5 + s]
        leaving += copies_in(
            [(ready.at[0, n], new_density.at[x]), (ready.at[pl.ds(1, species_n), n], mass.at[:, x])],
            out_semaphores.at[n],
        )
    for copy in leaving:
        copy.wait()


SPACES = {"h": pltpu.HBM, "v": pltpu.VMEM, "x": pltpu.HBM}


def placed_call(kernel, inputs, in_spaces, outputs, out_spaces, scratch, aliases={}):
    specs, operands = [], []
    for value, space in zip(inputs, in_spaces, strict=True):
        specs.append(pl.BlockSpec(memory_space=pl.ANY if space == "h" else pltpu.VMEM))
        if space != "-":
            value = pltpu.with_memory_space_constraint(value, SPACES[space])
        operands.append(value)
    shapes = []
    for shape, space in zip(outputs, out_spaces, strict=True):
        shape, kind = (shape, jnp.float32) if isinstance(shape, tuple) else (shape.shape, shape.dtype)
        shapes.append(jax.ShapeDtypeStruct(shape, kind) if space == "-" else SPACES[space](shape, kind))
    return pl.pallas_call(
        kernel,
        out_shape=shapes,
        in_specs=specs,
        out_specs=[pl.BlockSpec(memory_space=pl.ANY if space == "x" else pltpu.VMEM) for space in out_spaces],
        scratch_shapes=scratch,
        input_output_aliases=aliases,
        compiler_params=pltpu.CompilerParams(vmem_limit_bytes=GRANT),
    )(*operands)


def exchanged(value, axis, step):
    count = lax.axis_size(axis)
    return lax.ppermute(value, axis, [(i, partner(i, step, count)) for i in range(count)])


def partner(index, step, count):
    return index ^ step if count & (count - 1) == 0 else (index + step) % count


def target_of(index, step, count):
    return index ^ step if count & (count - 1) == 0 else lax.rem(index + step, count)


def source_of(index, step, count):
    return index ^ step if count & (count - 1) == 0 else lax.rem(index + count - step, count)


def face_roles(axis):
    if lax.axis_size(axis) % 2:
        return 0, 0
    second = lax.rem(lax.axis_index(axis), 2)
    return second, 1 - second


def faced_pairs(value, axis, first_round):
    count = lax.axis_size(axis)
    if count % 2:
        return shifted(value, axis, 1 if first_round else -1)
    start = 0 if first_round else 1
    pairs = [((start + i) % count, (start + i + 1) % count) for i in range(0, count, 2)]
    return lax.ppermute(value, axis, pairs + [(b, a) for a, b in pairs])


def shifted(value, axis, step):
    count = lax.axis_size(axis)
    return lax.ppermute(value, axis, [(i, (i + step) % count) for i in range(count)])


def hartley(rows, columns, length):
    angle = 2.0 * np.pi / length * (np.outer(rows, columns) % length)
    return np.cos(angle) + np.sin(angle)


def curvature(length):
    return 4.0 * np.sin(np.pi / length * np.arange(length)) ** 2


def decay_tables(nx, ny, nz):
    mu = curvature(nz)[:, None] + curvature(ny)[None, :]
    mu[0, 0] = 1.0
    root = np.sqrt(mu * (4.0 + mu))
    decay = 2.0 / (2.0 + mu + root)
    return np.stack([decay, 1.0 / (1.0 - decay**nx), -1.0 / (root * ny * nz)]).astype(np.float32)


def flat_mode_table(block, nx, ny, nz):
    rows = -(-(block + 2) // 8) * 8
    cell = np.arange(-1, rows - 1)[:, None]
    segment = np.arange(nx // block)[:, None]
    source = (np.arange(block)[None, :] - block * segment).reshape(1, -1)
    gap = (cell - source) % nx
    table = gap * (nx - gap) / (2.0 * nx) - (nx * nx - 1.0) / (12.0 * nx)
    return (table / (ny * nz)).astype(np.float32)


def segments(kz, width):
    return lax.broadcasted_iota(jnp.int32, (kz, LANES), 1) // width


def turned(value, lanes):
    lanes = lanes % LANES
    return pltpu.roll(value, lanes, 1) if lanes else value


def along_y_kernel(count, block, *rest):
    received, (table_y, tables, modes, sums, grid_rows, lines) = rest[:count], rest[count:]
    for step in range(count):
        lines[source_of(lax.axis_index("hy"), step, count)] = received[step][...]
    kz = lines.shape[1]
    nx, _, ny = modes.shape
    width = block
    per = LANES // width
    place = segments(kz, width)
    for column in range(ny // LANES):
        for high in range(nx // per):
            source = []
            for s in range(per):
                source.append(lines[column * per + s, :, high * LANES : (high + 1) * LANES])
            for low in range(per):
                line = turned(source[0], -low * width)
                for s in range(1, per):
                    line = jnp.where(place == s, turned(source[s], (s - low) * width), line)
                x = high * per + low
                grid_rows[x * kz : (x + 1) * kz, column * LANES : (column + 1) * LANES] = line
    spectrum = jnp.dot(
        grid_rows[...], table_y[...], precision=highest, preferred_element_type=jnp.float32
    )
    modes[...] = spectrum.reshape(nx, kz, ny)
    decay = tables[0]
    forward, backward = modes[0], modes[nx - 1]
    for x in range(1, nx):
        forward = forward * decay + modes[x]
        backward = backward * decay + modes[nx - 1 - x]
    sums[0:kz] = forward
    sums[kz : 2 * kz] = backward
    for x in range(nx):
        sums[2 * kz + x : 2 * kz + x + 1] = modes[x, 0:1, :]


def along_x_kernel(count, size_g, block, modes, own, *rest):
    others = rest[: count - 1]
    table_y, tables, flat_table, out, everyone, gathered, potential, lines, ready, semaphores = rest[count - 1 :]
    leaving = []
    me = lax.axis_index("hx")
    everyone[me] = own[...]
    for step in range(1, count):
        everyone[source_of(me, step, count)] = others[step - 1][...]

    def seen(distance):
        return everyone.at[lax.rem(me + count - distance, count)]

    nx, kz, ny = modes.shape
    width = block
    per = LANES // width
    for s in range(count):
        gathered[s * nx : (s + 1) * nx] = seen(s)[2 * kz : 2 * kz + nx]
    flat = jnp.dot(
        flat_table[...], gathered[...], precision=highest, preferred_element_type=jnp.float32
    )
    for tile in range(0, kz, 8):
        rows = slice(tile, tile + 8)
        decay, closing, scale = tables[0, rows], tables[1, rows], tables[2, rows]
        far = decay
        for _ in range(int(math.log2(nx))):
            far = far * far
        left = own[tile : tile + 8]
        right = own[kz + tile : kz + tile + 8]
        for s in range(count - 1, 0, -1):
            left = left * far + seen(s)[tile : tile + 8]
            right = right * far + seen(count - s)[kz + tile : kz + tile + 8]
        left, right = left * closing, right * closing
        from_left = [left]
        for x in range(nx):
            from_left.append(from_left[-1] * decay + modes[x, rows])
        result = [None] * (nx + 2)
        result[nx + 1] = from_left[nx] * decay + right
        behind = right
        for x in range(nx - 1, -1, -1):
            result[x + 1] = behind * decay + from_left[x + 1]
            behind = behind * decay + modes[x, rows]
        result[0] = from_left[0] + behind * decay
        if tile == 0:
            first = lax.broadcasted_iota(jnp.int32, (8, ny), 0) + lax.broadcasted_iota(jnp.int32, (8, ny), 1)
            first = first + place_in_plane()[1] == 0
        for x in range(nx + 2):
            value = result[x] * scale
            if tile == 0:
                value = jnp.where(first, flat[x : x + 1, :], value)
            potential[x * kz + tile : x * kz + tile + 8] = value
    lines[...] = jnp.dot(
        potential[...], table_y[...], precision=highest, preferred_element_type=jnp.float32
    )
    place = segments(kz, width)
    lane = lax.broadcasted_iota(jnp.int32, (kz, LANES), 1)

    def line(x, column):
        return lines[(x + 1) * kz : (x + 2) * kz, column * LANES : (column + 1) * LANES]

    for target in range(ny // width):
        column, s = target // per, target % per
        pieces = []
        for high in range(nx // per):
            piece = turned(line(high * per, column), -s * width)
            for low in range(1, per):
                piece = jnp.where(place == low, turned(line(high * per + low, column), (low - s) * width), piece)
            pieces.append(piece)
        edge = turned(line(-1, column), -s * width)
        edge = jnp.where(place == 1, turned(line(nx, column), (1 - s) * width), edge)
        for side, y in enumerate((target * width - 1, (target + 1) * width)):
            y = y % ny
            for x in range(nx):
                slot = 2 * width + side * nx + x
                edge = jnp.where(lane == slot, turned(line(x, y // LANES), slot - y % LANES), edge)
        pieces.append(edge)
        for p, piece in enumerate(pieces):
            ready[target, :, p * LANES : (p + 1) * LANES] = piece
        leaving += copies_in(
            [(ready.at[target], out.at[target * size_g + g]) for g in range(size_g)], semaphores.at[target]
        )
    for copy in leaving:
        copy.wait()


def gravity_kernel(planes, table, den, vel, carried, carried_rim, potential, momentum, energy, solved, edges, ready, semaphores):
    nx, ny, nz = den.shape
    groups, kz, width = planes.shape
    main = nx * ny
    flat = planes[...].reshape(groups * kz, width)
    here = table[...]
    contract = (((0,), (0,)), ((), ()))
    solved[...] = lax.dot_general(
        flat[:, :main], here, contract, precision=highest, preferred_element_type=jnp.float32
    )
    edges[...] = lax.dot_general(
        flat[:, main:], here[:, :nz], contract, precision=highest, preferred_element_type=jnp.float32
    )
    leaving = []
    row = lax.broadcasted_iota(jnp.int32, (ny, nz), 0)
    for x in range(nx):
        value = solved[x * ny : (x + 1) * ny, :nz]
        ready[4, x] = value
        above = solved[(x + 1) * ny : (x + 2) * ny, :nz] if x < nx - 1 else edges[ny : 2 * ny]
        below = solved[(x - 1) * ny : x * ny, :nz] if x > 0 else edges[:ny]
        at = 2 * ny + x
        right = jnp.where(row == ny - 1, edges[at + nx : at + nx + 1], pltpu.roll(value, ny - 1, 0))
        left = jnp.where(row == 0, edges[at : at + 1], pltpu.roll(value, 1, 0))
        pull = time_step * den[x]
        kicks = [
            pull * (-0.5 * (above - below)),
            pull * (-0.5 * (right - left)),
            pull * solved[x * ny : (x + 1) * ny, nz:],
        ]
        before = [carried_rim[d, x // (nx - 1)] if x in (0, nx - 1) else carried[d, x] for d in range(4)]
        work = before[3]
        for d in range(3):
            ready[d, x] = before[d] + kicks[d]
            work = work + kicks[d] * vel[d, x]
        ready[3, x] = work
        if x % 2:
            pair = pl.ds(x - 1, 2)
            leaving += copies_in(
                [
                    (ready.at[pl.ds(0, 3), pair], momentum.at[:, pair]),
                    (ready.at[3, pair], energy.at[pair]),
                    (ready.at[4, pair], potential.at[pair]),
                ],
                semaphores.at[x // 2],
            )
    for copy in leaving:
        copy.wait()


def step(density, velocity, pressure, species, newton_count):
    size_x, size_y, size_g = (lax.axis_size(a) for a in ("hx", "hy", "ga"))
    nx, ny, nz = density.shape
    all_x, all_y, all_z = nx * size_x, ny * size_y, nz * size_g
    groups = size_y * size_g
    kz = all_z // groups
    main = nx * ny
    width = main + LANES

    keys_z = np.arange(all_z)
    table_z = hartley(keys_z, keys_z, all_z)
    ahead = hartley(keys_z, keys_z + 1, all_z)
    behind = hartley(keys_z, keys_z - 1, all_z)
    into_z = table_z.reshape(size_g, all_z // size_g, size_g, nz).transpose(0, 2, 1, 3)
    into_z = jnp.asarray(into_z, jnp.float32)
    pull_z = -0.5 * (ahead - behind)
    from_z = np.concatenate(
        [t.reshape(all_z, size_g, nz).transpose(1, 0, 2) for t in (table_z, pull_z)], axis=2
    )
    from_z = from_z.reshape(size_g, size_g, size_y, kz, 2 * nz).transpose(0, 2, 1, 3, 4)
    from_z = jnp.asarray(from_z.reshape(size_g, all_z, 2 * nz), jnp.float32)
    keys_y = np.arange(all_y)
    table_y = jnp.asarray(hartley(keys_y, keys_y, all_y), jnp.float32)
    tables = jnp.asarray(decay_tables(all_x, all_y, all_z))
    flat_table = jnp.asarray(flat_mode_table(nx, all_x, all_y, all_z))

    floats = functools.partial(pltpu.VMEM, dtype=jnp.float32)

    near_density = [exchanged(density, "ga", step) for step in range(1, size_g)]
    into, den, vel, cooled, dense, sound, xfirst, xlast, ylo, yhi, zface, own_y, own_decay, own_flat = placed_call(
        pack_kernel,
        (density, velocity, pressure, species, newton_count, into_z, table_y, tables, flat_table),
        "hhhhhhhhh",
        [into_z.shape[1:], density.shape, velocity.shape, pressure.shape, species.shape, density.shape]
        + [(prim_n, ny, nz)] * 2 + [(prim_n, nx, nz)] * 2 + [(nx, ny, LANES)]
        + [table_y.shape, (3, kz, all_y), flat_table.shape],
        OUT_PACK,
        [
            pltpu.VMEM((nx, ny, nz), jnp.int32),
            pltpu.SemaphoreType.DMA((2, 5)),
            pltpu.SemaphoreType.DMA((4,)),
        ],
    )
    spectral = placed_call(
        functools.partial(along_z_kernel, size_g, size_y),
        (den, *near_density, into),
        "v" + "-" * (size_g - 1) + "v",
        [(kz, main)] * size_y,
        "-" * size_y,
        [floats((all_z // size_g, main))],
    )
    spectral = list(spectral)
    for step in range(1, size_y):
        spectral[step] = exchanged(spectral[step], "hy", step)
    modes, sums = placed_call(
        functools.partial(along_y_kernel, size_y, ny),
        (*spectral, own_y, own_decay),
        "-" * size_y + "vv",
        [(nx, kz, all_y), (2 * kz + nx, all_y)],
        OUT_Y,
        [floats((nx * kz, all_y)), floats((size_y, kz, main))],
    )
    ybelow = shifted(yhi, "hy", 1)
    yabove = shifted(ylo, "hy", -1)
    zbelow = shifted(zface, "ga", 1)
    zabove = zbelow if size_g == 2 else shifted(zface, "ga", -1)
    others = []
    for step in range(1, size_x):
        others.append(exchanged(sums, "hx", step))
    xfirst = faced_pairs(xfirst, "hx", True)
    xlast = faced_pairs(xlast, "hx", False)
    (planes,) = placed_call(
        functools.partial(along_x_kernel, size_x, size_g, ny),
        (modes, sums, *others, own_y, own_decay, own_flat),
        "v-" + IN_OTHERS * (size_x - 1) + "vvv",
        [(groups, kz, width)],
        OUT_X,
        [
            floats((size_x, 2 * kz + nx, all_y)),
            floats((all_x, all_y)),
            floats(((nx + 2) * kz, all_y)),
            floats(((nx + 2) * kz, all_y)),
            floats((size_y, kz, width)),
            pltpu.SemaphoreType.DMA((size_y, size_g)),
        ],
    )
    planes = lax.all_to_all(planes, ("hy", "ga"), split_axis=0, concat_axis=0, tiled=True)
    state = (den, vel, cooled, dense, sound)
    new_density, species_mass, carried, rim, own_z = placed_call(
        flux_kernel,
        (*state, ybelow, yabove, zbelow, zabove, from_z),
        IN_FLUX,
        [
            (nx, ny, nz), (species_n, nx, ny, nz), (4, nx, ny, nz),
            (prim_n, 2, ny, nz), from_z.shape[1:],
        ],
        OUT_FLUX,
        [
            floats((1 + species_n, nx - 2, ny, nz)),
            floats((2, flow_n, nx, nz)),
            pltpu.SemaphoreType.DMA((2, nx - 2)),
            pltpu.SemaphoreType.DMA((1,)),
        ],
    )
    new_density, species_mass, carried_rim = placed_call(
        rim_kernel,
        (*state, rim, xfirst, xlast, new_density, species_mass),
        IN_RIM,
        [(nx, ny, nz), (species_n, nx, ny, nz), (4, 2, ny, nz)],
        OUT_RIM,
        [
            floats((2, prim_n, ny, nz)),
            floats((1 + species_n, 2, ny, nz)),
            pltpu.SemaphoreType.DMA((2,)),
            pltpu.SemaphoreType.DMA((2, 2)),
        ],
        {8: 0, 9: 1},
    )
    potential, momentum, total_energy = placed_call(
        gravity_kernel,
        (planes, own_z, den, vel, carried, carried_rim),
        IN_GRAVITY,
        [(nx, ny, nz), (3, nx, ny, nz), (nx, ny, nz)],
        "xxx",
        [floats((main, 2 * nz)), floats((LANES, nz)), floats((5, nx, ny, nz)), pltpu.SemaphoreType.DMA((nx // 2, 3))],
    )
    return (new_density, momentum, total_energy, species_mass, potential)


def solution(mesh):
    cells = P("hx", "hy", "ga")
    fields = P(None, "hx", "hy", "ga")
    return jax.shard_map(
        step,
        mesh=mesh,
        in_specs=(cells, fields, cells, fields, cells),
        out_specs=(cells, fields, cells, fields, cells),
        check_vma=False,
    )
```
